128 devices in a mesh: brick: 16 (over z, y), narrow: 8 (over x, core).
Axes of the slice: x: 4, y: 4, z: 4, core: 2. Of those that a mesh axis runs over, the one named last changes fastest.
Arguments:
- potential: float32 [64, 32, 128], P('brick', 'narrow'), may hold values from -1 to 1
- functions: bfloat16 [16, 8, 64, 8, 8, 128], P('brick', 'narrow'), may hold values from -6 to 6
- kernel_store: bfloat16 [32768, 1152], P(('brick', 'narrow')), may hold values from -0.25 to 0.25
- owners: int32 [4096, 1], P(('brick', 'narrow')), may hold values from 0 to 127; in each aligned block of 32 rows (0 to 31, 32 to 63, ...) at most 2 rows name the same one
Outputs:
- pair_blocks: float32 [32768, 2, 1152], P(('brick', 'narrow'))
- gradients: bfloat16 [16, 8, 64, 8, 8, 128], P('brick', 'narrow')
The draws below stay inside these ranges and needn't reach their ends.
Inputs may be any that keep to these rules, and one draw needn't show every extreme that they name: `owners`: no more than 2 atoms of one brick share an owner, and in every draw some brick has exactly 2 atoms with one owner.
All inputs are finite; a program needn't handle non-finite values.
Results may differ from the reference program's by a relative error of at most 0.001.
Values may be sent and summed in bfloat16 or wider, within the bound.
No kernel may reach another device: no remote copies, remote signals or barrier semaphores. Data moves between devices by JAX's collectives and lax.ppermute only.
A program may use at most 64 MiB of HBM per device.

```python
import math
import jax
import jax.numpy as jnp
import numpy as np
from jax import lax

AD = 32
BX = 4
BY = 4
BZ = 128
W = 2
FD = 64
EX = 8
EY = 8
ROW = 1152
CAP = 2
SLOTS = 256
ATOMS = 4096
NX = 64
NY = 32
N_BRICK = 16
N_NARROW = 8
DEVICES = 128


def shard_levels(own_key, dims, shards, least, largest):
    def one(dim, blocks):
        heights = jax.random.uniform(jax.random.fold_in(jax.random.fold_in(own_key, 6), dim), (blocks,), jnp.float32, least / len(shards), largest / len(shards))
        return jnp.repeat(jnp.exp(heights), dims[dim] // blocks).reshape((-1,) + (1,) * (len(dims) - dim - 1))

    gain = one(*shards[0])
    for cut in shards[1:]:
        gain = gain * one(*cut)
    return gain


def shared_out(stream_key, own, number, rows, amount, top, bound, lean):
    sequence = jax.random.permutation(stream_key, amount)
    heavy_load, ordinary = portions_of(amount, rows * top, bound, lean, True), portions_of(amount, rows * top, bound, lean, False)
    places = jnp.arange(amount)

    def named(sizes, offset_by):
        used = int((sizes > 0).sum())
        fixed = max(1, used // 4)
        passed = fixed + (places - fixed + offset_by * (used - fixed)) % max(1, amount - fixed)
        return jnp.zeros((amount,), jnp.int32).at[sequence[jnp.where(places < fixed, places, passed)]].set(jnp.asarray(sizes, jnp.int32))

    sizes = jnp.where(number % 4 == 0, named(heavy_load, number // 4), named(ordinary, number - number // 4 - 1))
    mixed = jax.random.permutation(jax.random.fold_in(own, 3), amount)
    donor, sink = mixed[0:amount // 2 * 2:2], mixed[1:amount // 2 * 2:2]
    room = jnp.minimum(sizes[donor] - 1, bound - sizes[sink]) // 2
    room = jnp.where((donor == sequence[0]) | (sink == sequence[0]) | (sizes[sink] == 0), 0, jnp.maximum(room, 0))
    passed = jax.random.randint(jax.random.fold_in(own, 4), (amount // 2,), 0, 1 << 20) % (room + 1)
    sizes = sizes.at[donor].add(-passed).at[sink].add(passed)
    labels = jnp.searchsorted(jnp.cumsum(sizes), jnp.arange(rows * top), side="right").astype(jnp.int32)
    table = labels.reshape(top, rows).T
    table = table[jax.random.permutation(jax.random.fold_in(own, 1), rows)]
    offset_by = jax.random.randint(jax.random.fold_in(own, 2), (rows, 1), 0, top)
    return jnp.take_along_axis(table, (jnp.arange(top)[None, :] + offset_by) % top, axis=1)


def portions_of(amount, total, most, skew, full):
    weights = [(1 << 20) // math.isqrt(standing ** skew) + 1 for standing in range(1, amount + 1)]
    largest = most if full else min(most, max(-(-total // amount), total * weights[0] // sum(weights)))
    least = 1 if total - largest >= amount - 1 else 0
    holding, rest = [largest] + [least] * (amount - 1), total - largest - least * (amount - 1)
    while rest > 0:
        free = [i for i in range(1, amount) if holding[i] < largest] or [i for i in range(1, amount) if holding[i] < most]
        mass, budget = sum([weights[i] for i in free]), rest
        for i in free:
            addition = min(most - holding[i], max(1, budget * weights[i] // mass), rest)
            holding[i] = holding[i] + addition
            rest = rest - addition
    return np.array(holding)


def bell_draw(stream_key, shape, spread, limit, shards=(), kind=jnp.bfloat16):
    values = spread * jax.random.normal(stream_key, shape, jnp.float32)
    if shards:
        values = values * shard_levels(stream_key, shape, shards, -0.22, 0.18)
    return jnp.clip(values, -limit, limit).astype(kind)


def setup_inputs(seed: int = 0) -> dict:
    arg_keys = jax.random.split(jax.random.key(seed), 5)
    potential = jnp.clip(jax.random.uniform(arg_keys[0], (NX, NY, BZ), jnp.float32, -1.0, 1.0) * shard_levels(arg_keys[0], (NX, NY, BZ), ((0, 16), (1, 8)), -0.4, 0.0), -1.0, 1.0)
    functions = bell_draw(arg_keys[1], (N_BRICK, N_NARROW, FD, EX, EY, BZ), 1.0, 6.0, ((0, 16), (1, 8)))
    kernel_store = bell_draw(arg_keys[2], (DEVICES * SLOTS, ROW), (9 * FD) ** -0.5, 0.25, ((0, 128),))
    owners_keys = jax.random.split(jax.random.fold_in(arg_keys[3], 1), ATOMS // AD)
    owners_turns = jax.random.permutation(jax.random.fold_in(arg_keys[3], 3), ATOMS // AD)
    owners = jax.vmap(lambda own, number: shared_out(jax.random.fold_in(arg_keys[3], 2), own, number, AD, DEVICES, 1, CAP, 2))(owners_keys, owners_turns).reshape((ATOMS, 1))
    return dict(potential=potential, functions=functions, kernel_store=kernel_store, owners=owners)


OFFSETS = ((0, 0), (1, 0), (-1, 0), (0, 1), (0, -1), (1, 1), (1, -1), (-1, 1), (-1, -1))


def apply_ham(values, box_pot):
    padded = jnp.pad(values, ((0, 0), (1, 1), (1, 1), (1, 1)))
    beside = padded[:, 2:, 1:-1, 1:-1] + padded[:, :-2, 1:-1, 1:-1]
    beside = beside + padded[:, 1:-1, 2:, 1:-1] + padded[:, 1:-1, :-2, 1:-1]
    beside = beside + padded[:, 1:-1, 1:-1, 2:] + padded[:, 1:-1, 1:-1, :-2]
    return (3.0 + box_pot)[None] * values - 0.5 * beside


def near_cut(step, extent, band_width):
    if step == 0:
        return slice(0, extent)
    if step == 1:
        return slice(extent - band_width, extent)
    return slice(0, band_width)


def far_cut(step, extent, band_width):
    if step == 0:
        return slice(0, extent)
    if step == 1:
        return slice(0, band_width)
    return slice(extent - band_width, extent)


def reference(potential, functions, kernel_store, owners):
    band_width = 2 * W
    cell_volume = 1.0 / (EX * EY * BZ)
    wrapped = jnp.pad(potential, ((W, W), (W, W), (0, 0)), mode="wrap")
    owner_col = owners[:, 0]

    def per_brick(source):
        brick_x = source // N_NARROW
        brick_y = source % N_NARROW
        box_pot = lax.dynamic_slice(wrapped, (brick_x * BX, brick_y * BY, jnp.int32(0)), (EX, EY, BZ))
        own_funcs = functions[brick_x, brick_y]
        applied = apply_ham(own_funcs.astype(jnp.float32), box_pot).astype(jnp.bfloat16)
        own_owner = lax.dynamic_slice_in_dim(owner_col, source * AD, AD)
        atom_order = jnp.arange(AD, dtype=jnp.int32)
        earlier = (own_owner[:, None] == own_owner[None, :]) & (atom_order[None, :] < atom_order[:, None])
        atom_rank = jnp.sum(earlier.astype(jnp.int32), axis=1)
        slot_of = own_owner * SLOTS + source * CAP + atom_rank
        kernel_mat = jnp.take(kernel_store, slot_of, axis=0).reshape(FD, 9, FD)
        s_parts = []
        h_parts = []
        mixed = jnp.zeros((FD, EX, EY, BZ), jnp.float32)
        for position, (step_x, step_y) in enumerate(OFFSETS):
            partner = functions[(brick_x + step_x) % N_BRICK, (brick_y + step_y) % N_NARROW]
            far_piece = partner[:, far_cut(step_x, EX, band_width), far_cut(step_y, EY, band_width)]
            cut_x = near_cut(step_x, EX, band_width)
            cut_y = near_cut(step_y, EY, band_width)
            far_flat = far_piece.reshape(FD, -1)
            near_flat = own_funcs[:, cut_x, cut_y].reshape(FD, -1)
            applied_flat = applied[:, cut_x, cut_y].reshape(FD, -1)
            s_parts.append(jnp.dot(near_flat, far_flat.T, preferred_element_type=jnp.float32) * cell_volume)
            h_parts.append(jnp.dot(applied_flat, far_flat.T, preferred_element_type=jnp.float32) * cell_volume)
            added = jnp.dot(kernel_mat[:, position], far_flat, preferred_element_type=jnp.float32)
            mixed = mixed.at[:, cut_x, cut_y].add(added.reshape(far_piece.shape))
        gradient = apply_ham(mixed, box_pot).astype(jnp.bfloat16)
        intersection_rows = jnp.stack(s_parts, axis=1).reshape(AD, ROW)
        ham_rows = jnp.stack(h_parts, axis=1).reshape(AD, ROW)
        pair_rows = jnp.stack([intersection_rows, ham_rows], axis=1)
        return pair_rows, slot_of, gradient

    pair_rows, slots_all, gradients = lax.map(per_brick, jnp.arange(DEVICES, dtype=jnp.int32))
    pair_blocks = jnp.zeros((DEVICES * SLOTS, 2, ROW), jnp.float32)
    pair_blocks = pair_blocks.at[slots_all.reshape(-1)].set(pair_rows.reshape(-1, 2, ROW))
    gradients = gradients.reshape(N_BRICK, N_NARROW, FD, EX, EY, BZ)
    return pair_blocks, gradients
```

```python
import functools

import jax
import jax.numpy as jnp
from jax import lax
from jax.experimental import pallas as pl
from jax.experimental.pallas import tpu as pltpu
from jax.sharding import PartitionSpec as P

AT_X = {1: 1, 0: 2}
AT_Y = {1: 3, 0: 4}
AT_XY = {(1, 1): 5, (1, 0): 6, (0, 1): 7, (0, 0): 8}
SIDES = ((0, 0), (0, 1), (1, 0), (1, 1))
HEADROOM = 14
VMEM = pl.BlockSpec(memory_space=pltpu.VMEM)
SMEM = pl.BlockSpec(memory_space=pltpu.SMEM)


def shifted(shard, axis, by):
    size = lax.axis_size(axis)
    return lax.ppermute(shard, axis, [(i, (i + by) % size) for i in range(size)])


def params(mib=48):
    return pltpu.CompilerParams(vmem_limit_bytes=mib << 20)


def split_kernel(half, f_ref, x0_ref, x1_ref, y0_ref, y1_ref):
    for x in range(2 * half):
        rows = jnp.swapaxes(f_ref[:, x], 0, 1)
        side_x, at = divmod(x, half)
        for side_y in (0, 1):
            part = rows[side_y * half : (side_y + 1) * half]
            (x0_ref, x1_ref)[side_x][side_y, at] = part
            (y0_ref, y1_ref)[side_y][side_x, at] = part


def pair_kernel(k_ref, o_ref):
    o_ref[...] = k_ref[...].reshape(o_ref.shape)


def stencil(cell, potential_row, half, x, y, zero_low, zero_high):
    value = cell(x, y)
    beside = jnp.where(zero_high, 0.0, pltpu.roll(value, value.shape[1] - 1, 1)) + jnp.where(
        zero_low, 0.0, pltpu.roll(value, 1, 1)
    )
    for near_x, near_y in ((x + 1, y), (x - 1, y), (x, y + 1), (x, y - 1)):
        if 0 <= near_x < 2 * half and 0 <= near_y < 2 * half:
            beside = beside + cell(near_x, near_y)
    return (3.0 + potential_row(x, y)) * value - 0.5 * beside


def potential_rows(low_ref, mid_ref, high_ref):
    margin = low_ref.shape[1]
    inner = mid_ref.shape[1]

    def row(x, y):
        if y < margin:
            return low_ref[x, y : y + 1]
        if y < margin + inner:
            return mid_ref[x, y - margin : y - margin + 1]
        return high_ref[x, y - margin - inner : y - margin - inner + 1]

    return row


def edges(func_count, depth):
    lane = lax.broadcasted_iota(jnp.int32, (func_count, depth), 1)
    return lane == 0, lane == depth - 1


def ranks(owner_ref, count_ref):
    def clear(i, carry):
        count_ref[owner_ref[i]] = 0
        return carry

    lax.fori_loop(0, owner_ref.shape[0], clear, 0)
    found = []
    for a in range(owner_ref.shape[0]):
        owner = owner_ref[a]
        rank = count_ref[owner]
        count_ref[owner] = rank + 1
        found.append((owner, rank))
    return found


def pairs_kernel(half, cap, owner_ref, *refs):
    own, from_x, from_y, from_xy = refs[0:2], refs[2:4], refs[4:6], refs[6:10]
    row_of = potential_rows(*refs[10:13])
    out_ref, sums_ref, count_ref = refs[13:16]
    func_count, depth = own[0].shape[-2:]
    atoms = owner_ref.shape[0]
    low_edge, high_edge = edges(func_count, depth)

    def cell(x, y):
        side_x, at_x = divmod(x, half)
        side_y, at_y = divmod(y, half)
        return own[side_x][side_y, at_x, at_y].astype(jnp.float32)

    out_ref[...] = jnp.zeros(out_ref.shape, out_ref.dtype)
    block = {}
    for number, (side_x, side_y) in enumerate(SIDES):
        total = jnp.zeros((2 * func_count, 4 * func_count), jnp.float32)
        for at_x in range(half):
            left, right = [], []
            for at_y in range(half):
                near = own[side_x][side_y, at_x, at_y]
                applied = stencil(
                    cell, row_of, half, side_x * half + at_x, side_y * half + at_y, low_edge, high_edge
                ).astype(jnp.bfloat16)
                left.append(jnp.concatenate([near, applied], axis=0))
                right.append(
                    jnp.concatenate(
                        [
                            near,
                            from_x[side_x][side_y, at_x, at_y],
                            from_y[side_y][side_x, at_x, at_y],
                            from_xy[number][at_x, at_y],
                        ],
                        axis=0,
                    )
                )
            total = total + lax.dot_general(
                jnp.concatenate(left, axis=1),
                jnp.concatenate(right, axis=1),
                (((1,), (1,)), ((), ())),
                preferred_element_type=jnp.float32,
            )
        block[side_x, side_y] = total

    def columns(part, *sides):
        return functools.reduce(
            jnp.add, [block[s][:, part * func_count : (part + 1) * func_count] for s in sides]
        )

    parts = [columns(0, *SIDES)] + [None] * 8
    for side in (0, 1):
        parts[AT_X[side]] = columns(1, (side, 0), (side, 1))
        parts[AT_Y[side]] = columns(2, (0, side), (1, side))
    for sides in SIDES:
        parts[AT_XY[sides]] = columns(3, sides)
    width = 9 * func_count
    volume = 1.0 / (4 * half * half * depth)
    sums = jnp.concatenate(parts, axis=1) * volume
    for t in range(0, width, depth):
        sums_ref[t // depth, :, : min(depth, width - t)] = sums[:, t : t + depth]

    def atom_rows(start):
        picked = []
        for i in (0, 1):
            tiles = [sums_ref[t, pl.ds(start + i, atoms, stride=2), :] for t in range(sums_ref.shape[0])]
            picked.append(jnp.concatenate(tiles, axis=1)[:, :width])
        return jnp.concatenate(picked, axis=1)

    rows = [atom_rows(0), atom_rows(func_count)]
    largest = jnp.maximum(
        jnp.max(jnp.abs(rows[0]), axis=1, keepdims=True), jnp.max(jnp.abs(rows[1]), axis=1, keepdims=True)
    )
    power = jnp.ceil(jnp.log2(jnp.maximum(largest, 1e-33))) - HEADROOM
    scale = jnp.exp2(-power)
    tail = jnp.broadcast_to(power, (atoms, depth))
    rows = [jnp.concatenate([r * scale, tail], axis=1) for r in rows]
    for a, (owner, rank) in enumerate(ranks(owner_ref, count_ref)):
        slot = owner * cap + rank
        out_ref[slot, 0:1, :] = rows[0][a : a + 1]
        out_ref[slot, 1:2, :] = rows[1][a : a + 1]


def mix_kernel(half, owner_ref, kernel_ref, *refs):
    own, from_x, from_y, from_xy = refs[0:2], refs[2:4], refs[4:6], refs[6:10]
    row_of = potential_rows(*refs[10:13])
    out_ref, rows_ref, mixed_ref, count_ref = refs[13:17]
    func_count, depth = own[0].shape[-2:]
    atoms = owner_ref.shape[0]
    low_edge, high_edge = edges(func_count, depth)
    for a, (owner, rank) in enumerate(ranks(owner_ref, count_ref)):
        both = kernel_ref[owner].astype(jnp.float32)
        rows_ref[a : a + 1, :] = jnp.where(rank == 0, both[0:1], both[1:2])
    width = 9 * func_count
    matrix = jnp.concatenate([rows_ref[:, :width], rows_ref[:, width:]], axis=0)
    for number, (side_x, side_y) in enumerate(SIDES):
        at = (0, AT_X[side_x], AT_Y[side_y], AT_XY[side_x, side_y])
        left = jnp.concatenate(
            [matrix[:, k * func_count : (k + 1) * func_count] for k in at], axis=1
        ).astype(jnp.bfloat16)
        for at_x in range(half):
            for at_y in range(0, half, 2):
                right = jnp.concatenate(
                    [
                        jnp.concatenate(
                            [
                                own[side_x][side_y, at_x, y],
                                from_x[side_x][side_y, at_x, y],
                                from_y[side_y][side_x, at_x, y],
                                from_xy[number][at_x, y],
                            ],
                            axis=0,
                        )
                        for y in (at_y, at_y + 1)
                    ],
                    axis=1,
                )
                got = jnp.dot(left, right, preferred_element_type=jnp.float32)
                for i in (0, 1):
                    mixed_ref[side_x * half + at_x, side_y * half + at_y + i] = got[
                        :, i * depth : (i + 1) * depth
                    ]

    def cell(x, y):
        return mixed_ref[x, y]

    for x in range(2 * half):
        made = [
            stencil(cell, row_of, half, x, y, low_edge, high_edge) for y in range(2 * half)
        ]
        for odd in (0, 1):
            stacked = jnp.stack([m[odd * atoms : (odd + 1) * atoms] for m in made], axis=0)
            out_ref[:, odd, x] = jnp.swapaxes(stacked, 0, 1).astype(out_ref.dtype)


def body(potential, functions, kernel_store, owners):
    own_funcs = functions[0, 0]
    func_count, ext_x, ext_y, depth = own_funcs.shape
    half = ext_x // 2
    margin = (ext_x - potential.shape[0]) // 2
    device_count = lax.axis_size("brick") * lax.axis_size("narrow")
    owner_col = owners[:, 0]
    atoms = owner_col.shape[0]
    slot_count, row_width = kernel_store.shape
    slot_cap = slot_count // device_count
    bf16 = jnp.bfloat16
    struct = jax.ShapeDtypeStruct

    band = struct((2, half, half, func_count, depth), bf16)
    own_x0, own_x1, own_y0, own_y1 = pl.pallas_call(
        functools.partial(split_kernel, half),
        out_shape=(band,) * 4,
        in_specs=[VMEM],
        out_specs=(VMEM,) * 4,
        compiler_params=params(),
        cost_estimate=pl.CostEstimate(flops=0, transcendentals=0, bytes_accessed=3 << 20),
    )(own_funcs)

    from_x = (shifted(own_x1, "brick", 1), shifted(own_x0, "brick", -1))
    from_y = (shifted(own_y1, "narrow", 1), shifted(own_y0, "narrow", -1))
    from_xy = [shifted(from_x[sx][1 - sy], "narrow", -1 if sy else 1) for sx, sy in SIDES]

    low = shifted(potential[-margin:], "brick", 1)
    high = shifted(potential[:margin], "brick", -1)
    middle = jnp.concatenate([low, potential, high], axis=0)
    low = shifted(middle[:, -margin:], "narrow", 1)
    high = shifted(middle[:, :margin], "narrow", -1)
    pots = (low, middle, high)

    kernel_out = pl.pallas_call(
        pair_kernel,
        out_shape=struct((device_count, slot_cap, row_width), bf16),
        in_specs=[VMEM],
        out_specs=VMEM,
        compiler_params=params(),
        cost_estimate=pl.CostEstimate(flops=0, transcendentals=0, bytes_accessed=1 << 20),
    )(kernel_store)
    kernel_in = lax.all_to_all(
        kernel_out, ("brick", "narrow"), split_axis=0, concat_axis=0, tiled=True
    )

    boxes = (own_x0, own_x1, *from_x, *from_y, *from_xy)
    cells = ext_x * ext_y * depth
    outgoing = pl.pallas_call(
        functools.partial(pairs_kernel, half, slot_cap),
        out_shape=struct((slot_count, 2, row_width + depth), jnp.float32),
        in_specs=[SMEM] + [VMEM] * 13,
        out_specs=VMEM,
        scratch_shapes=[
            pltpu.VMEM((pl.cdiv(9 * func_count, depth), 2 * func_count, depth), jnp.float32),
            pltpu.SMEM((device_count,), jnp.int32),
        ],
        compiler_params=params(),
        cost_estimate=pl.CostEstimate(
            flops=16 * func_count * func_count * cells, transcendentals=0, bytes_accessed=7 << 20
        ),
    )(owner_col, *boxes, *pots)
    blocks = lax.all_to_all(
        outgoing.astype(jnp.float16), ("brick", "narrow"), split_axis=0, concat_axis=0, tiled=True
    )
    power = blocks[:, :, row_width : row_width + 1].astype(jnp.float32)
    blocks = blocks[:, :, :row_width].astype(jnp.float32) * jnp.exp2(power)

    gradient = pl.pallas_call(
        functools.partial(mix_kernel, half),
        out_shape=struct((atoms, 2, ext_x, ext_y, depth), bf16),
        in_specs=[SMEM] + [VMEM] * 14,
        out_specs=VMEM,
        scratch_shapes=[
            pltpu.VMEM((atoms, row_width), jnp.float32),
            pltpu.VMEM((ext_x, ext_y, func_count, depth), jnp.float32),
            pltpu.SMEM((device_count,), jnp.int32),
        ],
        compiler_params=params(),
        cost_estimate=pl.CostEstimate(
            flops=8 * func_count * func_count * cells, transcendentals=0, bytes_accessed=7 << 20
        ),
    )(owner_col, kernel_in, *boxes, *pots)
    return (blocks, gradient.reshape(functions.shape))


def solution(mesh):
    in_specs = (
        P("brick", "narrow", None),
        P("brick", "narrow", None, None, None, None),
        P(("brick", "narrow"), None),
        P(("brick", "narrow"), None),
    )
    out_specs = (P(("brick", "narrow"), None, None), P("brick", "narrow", None, None, None, None))
    return jax.shard_map(body, mesh=mesh, in_specs=in_specs, out_specs=out_specs, check_vma=False)
```

```python
import functools

import jax
import jax.numpy as jnp
from jax import lax
from jax.experimental import pallas as pl
from jax.experimental.pallas import tpu as pltpu
from jax.sharding import PartitionSpec as P

AT_X = {1: 1, 0: 2}
AT_Y = {1: 3, 0: 4}
AT_XY = {(1, 1): 5, (1, 0): 6, (0, 1): 7, (0, 0): 8}
SIDES = ((0, 0), (0, 1), (1, 0), (1, 1))
STEPS = 64.0
TOP = 32700.0
SMALLEST = 1e-33
VMEM = pl.BlockSpec(memory_space=pltpu.VMEM)
SMEM = pl.BlockSpec(memory_space=pltpu.SMEM)


def shifted(shard, axis, by):
    size = lax.axis_size(axis)
    return lax.ppermute(shard, axis, [(i, (i + by) % size) for i in range(size)])


def params(mib=16):
    return pltpu.CompilerParams(vmem_limit_bytes=mib << 20)


def packed_rows(rows, func_count):
    value = jnp.concatenate(rows, axis=0)
    pieces = []
    for _ in range(3):
        piece = value.astype(jnp.bfloat16).astype(jnp.float32)
        pieces.append(piece)
        value = value - piece
    count = func_count - 3 * len(rows)
    pieces.append(jnp.zeros((count, value.shape[1]), jnp.float32))
    return jnp.concatenate(pieces, axis=0).astype(jnp.bfloat16)


def unpacked_rows(block, count):
    block = block.astype(jnp.float32)
    return block[:count] + block[count : 2 * count] + block[2 * count : 3 * count]


def split_x_kernel(half, f_ref, pot_ref, *out_refs):
    count = half * half
    func_count = f_ref.shape[0]
    inner = pot_ref.shape[0]
    margin = half - inner // 2
    for x in range(2 * half):
        rows = jnp.swapaxes(f_ref[:, x], 0, 1)
        side, at = divmod(x, half)
        for y in (0, 1):
            start = y * (count + 1) + at * half
            out_refs[side][start : start + half] = rows[y * half : (y + 1) * half]
    for side in (0, 1):
        first = side * (inner - margin)
        out_refs[side][count] = packed_rows(
            [pot_ref[first + i, j : j + 1] for i in range(margin) for j in range(inner)], func_count
        )


def split_y_kernel(half, x0_ref, x1_ref, pot_ref, *out_refs):
    count = half * half
    func_count = x0_ref.shape[1]
    inner = pot_ref.shape[0]
    margin = half - inner // 2
    for side in (0, 1):
        for side_x, x_ref in enumerate((x0_ref, x1_ref)):
            start, taken = side_x * (count + 1), side * (count + 1)
            out_refs[side][start : start + count] = x_ref[taken : taken + count]
        first = side * (inner - margin)
        out_refs[side][count] = packed_rows(
            [pot_ref[i, first + j : first + j + 1] for i in range(inner) for j in range(margin)], func_count
        )


class Boxes:
    def __init__(self, half, refs, pot_ref):
        self.half, self.count = half, half * half
        self.own, self.x, self.y, self.xy = refs[0:2], refs[2:4], refs[4:6], dict(zip(SIDES, refs[6:10]))
        self.pot = pot_ref
        self.inner = pot_ref.shape[0]
        self.margin = half - self.inner // 2
        self.edge = {}

    def columns(self, sides, at_x, at_y):
        side_x, side_y = sides
        at = at_x * self.half + at_y
        return [
            self.own[side_x][side_y * (self.count + 1) + at],
            self.x[side_x][side_y * (self.count + 1) + at],
            self.y[side_y][side_x * (self.count + 1) + at],
            self.xy[sides][1 - side_y + at],
        ]

    def edge_row(self, key, row):
        if key not in self.edge:
            ref = self.xy[key] if isinstance(key, tuple) and key in self.xy else getattr(self, key[0])[key[1]]
            at = self.count
            if key in self.xy:
                at = self.count * key[1]
            self.edge[key] = unpacked_rows(ref[at], self.margin * self.inner)
        return self.edge[key][row : row + 1]

    def potential(self, x, y):
        inner, margin = self.inner, self.margin
        in_x, in_y = (margin <= v < margin + inner for v in (x, y))
        side_x, side_y = x // self.half, y // self.half
        near_x, near_y = x - side_x * (margin + inner), y - side_y * (margin + inner)
        if in_x and in_y:
            return self.pot[x - margin, y - margin : y - margin + 1]
        if in_y:
            return self.edge_row(("x", side_x), near_x * inner + y - margin)
        if in_x:
            return self.edge_row(("y", side_y), (x - margin) * margin + near_y)
        column = near_y if side_y else inner - margin + near_y
        return self.edge_row((side_x, side_y), near_x * inner + column)


def pair_kernel(k_ref, o_ref):
    o_ref[...] = k_ref[...].reshape(o_ref.shape)


def stencil(cell, potential_row, half, x, y, zero_low, zero_high):
    value = cell(x, y)
    beside = jnp.where(zero_high, 0.0, pltpu.roll(value, value.shape[1] - 1, 1)) + jnp.where(
        zero_low, 0.0, pltpu.roll(value, 1, 1)
    )
    for near_x, near_y in ((x + 1, y), (x - 1, y), (x, y + 1), (x, y - 1)):
        if 0 <= near_x < 2 * half and 0 <= near_y < 2 * half:
            beside = beside + cell(near_x, near_y)
    return (3.0 + potential_row(x, y)) * value - 0.5 * beside


def edges(func_count, depth):
    lane = lax.broadcasted_iota(jnp.int32, (func_count, depth), 1)
    return lane == 0, lane == depth - 1


def ranks(owner_ref, count_ref):
    def clear(i, carry):
        count_ref[owner_ref[i]] = 0
        return carry

    lax.fori_loop(0, owner_ref.shape[0], clear, 0)
    found = []
    for a in range(owner_ref.shape[0]):
        owner = owner_ref[a]
        rank = count_ref[owner]
        count_ref[owner] = rank + 1
        found.append((owner, rank))
    return found


def pairs_kernel(half, cap, owner_ref, pot_ref, *refs):
    out_ref, wide_ref, sums_ref, count_ref = refs[10:14]
    boxes = Boxes(half, refs[0:10], pot_ref)
    func_count, depth = refs[0].shape[-2:]
    atoms = owner_ref.shape[0]
    low_edge, high_edge = edges(func_count, depth)

    def cell(x, y):
        side_x, at_x = divmod(x, half)
        side_y, at_y = divmod(y, half)
        return boxes.columns((side_x, side_y), at_x, at_y)[0].astype(jnp.float32)

    wide_ref[...] = jnp.zeros(wide_ref.shape, wide_ref.dtype)
    block = {}
    for side_x, side_y in SIDES:
        total = jnp.zeros((2 * func_count, 4 * func_count), jnp.float32)
        for at_x in range(half):
            left, right = [], []
            for at_y in range(half):
                columns = boxes.columns((side_x, side_y), at_x, at_y)
                applied = stencil(
                    cell, boxes.potential, half, side_x * half + at_x, side_y * half + at_y, low_edge, high_edge
                ).astype(jnp.bfloat16)
                left.append(jnp.concatenate([columns[0], applied], axis=0))
                right.append(jnp.concatenate(columns, axis=0))
            total = total + lax.dot_general(
                jnp.concatenate(left, axis=1),
                jnp.concatenate(right, axis=1),
                (((1,), (1,)), ((), ())),
                preferred_element_type=jnp.float32,
            )
        block[side_x, side_y] = total

    def summed(part, *sides):
        return functools.reduce(
            jnp.add, [block[s][:, part * func_count : (part + 1) * func_count] for s in sides]
        )

    parts = [summed(0, *SIDES)] + [None] * 8
    for side in (0, 1):
        parts[AT_X[side]] = summed(1, (side, 0), (side, 1))
        parts[AT_Y[side]] = summed(2, (0, side), (1, side))
    for sides in SIDES:
        parts[AT_XY[sides]] = summed(3, sides)
    width = 9 * func_count
    volume = 1.0 / (4 * half * half * depth)
    sums = jnp.concatenate(parts, axis=1) * volume
    for t in range(0, width, depth):
        sums_ref[t // depth, :, : min(depth, width - t)] = sums[:, t : t + depth]

    def atom_rows(start):
        picked = []
        for i in (0, 1):
            tiles = [sums_ref[t, pl.ds(start + i, atoms, stride=2), :] for t in range(sums_ref.shape[0])]
            picked.append(jnp.concatenate(tiles, axis=1)[:, :width])
        return jnp.concatenate(picked, axis=1)

    coded = []
    for start in (0, func_count):
        row = atom_rows(start)
        largest = jnp.maximum(jnp.max(jnp.abs(row), axis=1, keepdims=True), SMALLEST)
        power = jnp.ceil(STEPS * jnp.log2(largest))
        coded.append((row * (TOP * jnp.exp2(-power / STEPS)), jnp.broadcast_to(power, (atoms, depth))))
    tiles = 2 * width // depth
    for a, (owner, rank) in enumerate(ranks(owner_ref, count_ref)):
        for m, (row, power) in enumerate(coded):
            for t in range(tiles):
                wide_ref[owner, pl.ds(rank * (2 * tiles) + 2 * t + m, 1), :] = row[
                    a : a + 1, t * depth : (t + 1) * depth
                ]
            wide_ref[owner, pl.ds(cap * 2 * tiles + 2 * rank + m, 1), :] = power[a : a + 1]
    for owner in range(out_ref.shape[0]):
        out_ref[owner] = jnp.round(wide_ref[owner]).astype(jnp.int32).astype(jnp.int16)


def unpack_kernel(cap, in_ref, out_ref):
    chunks, rows, depth = in_ref.shape
    data = rows - 2 * cap
    line = lax.broadcasted_iota(jnp.int32, (data, depth), 0)
    even = line % 2 == 0
    for c in range(chunks):
        values = in_ref[c].astype(jnp.int32).astype(jnp.float32)
        scale = jnp.exp2(values[data:] * (1.0 / STEPS)) * (1.0 / TOP)
        spread = jnp.where(even, scale[0:1], scale[1:2])
        for rank in range(1, cap):
            spread = jnp.where(
                line >= rank * (data // cap),
                jnp.where(even, scale[2 * rank : 2 * rank + 1], scale[2 * rank + 1 : 2 * rank + 2]),
                spread,
            )
        values = values[:data] * spread
        for rank in range(cap):
            for t in range(data // (2 * cap)):
                start = rank * (data // cap) + 2 * t
                out_ref[c * cap + rank, :, t * depth : (t + 1) * depth] = values[start : start + 2]


def mix_kernel(half, owner_ref, kernel_ref, pot_ref, *refs):
    out_ref, rows_ref, mixed_ref, count_ref, sems = refs[10:15]
    held = refs[15:25]
    copies = [pltpu.make_async_copy(refs[i], held[i], sems.at[i]) for i in range(10)]
    for copy in copies:
        copy.start()
    boxes = Boxes(half, held, pot_ref)
    func_count, depth = refs[0].shape[-2:]
    atoms = owner_ref.shape[0]
    low_edge, high_edge = edges(func_count, depth)
    for a, (owner, rank) in enumerate(ranks(owner_ref, count_ref)):
        both = kernel_ref[owner].astype(jnp.float32)
        rows_ref[a : a + 1, :] = jnp.where(rank == 0, both[0:1], both[1:2])
    width = 9 * func_count
    matrix = jnp.concatenate([rows_ref[:, :width], rows_ref[:, width:]], axis=0)
    for copy in copies:
        copy.wait()
    for side_x, side_y in SIDES:
        at = (0, AT_X[side_x], AT_Y[side_y], AT_XY[side_x, side_y])
        left = jnp.concatenate(
            [matrix[:, k * func_count : (k + 1) * func_count] for k in at], axis=1
        ).astype(jnp.bfloat16)
        for at_x in range(half):
            for at_y in range(0, half, 2):
                right = jnp.concatenate(
                    [
                        jnp.concatenate(boxes.columns((side_x, side_y), at_x, y), axis=0)
                        for y in (at_y, at_y + 1)
                    ],
                    axis=1,
                )
                got = jnp.dot(left, right, preferred_element_type=jnp.float32)
                for i in (0, 1):
                    mixed_ref[side_x * half + at_x, side_y * half + at_y + i] = got[
                        :, i * depth : (i + 1) * depth
                    ]

    def cell(x, y):
        return mixed_ref[x, y]

    for x in range(2 * half):
        made = [
            stencil(cell, boxes.potential, half, x, y, low_edge, high_edge) for y in range(2 * half)
        ]
        for odd in (0, 1):
            stacked = jnp.stack([m[odd * atoms : (odd + 1) * atoms] for m in made], axis=0)
            out_ref[:, odd, x] = jnp.swapaxes(stacked, 0, 1).astype(out_ref.dtype)


def body(potential, functions, kernel_store, owners):
    own_funcs = functions[0, 0]
    func_count, ext_x, ext_y, depth = own_funcs.shape
    half = ext_x // 2
    margin = (ext_x - potential.shape[0]) // 2
    device_count = lax.axis_size("brick") * lax.axis_size("narrow")
    owner_col = owners[:, 0]
    atoms = owner_col.shape[0]
    slot_count, row_width = kernel_store.shape
    slot_cap = slot_count // device_count
    bf16 = jnp.bfloat16
    struct = jax.ShapeDtypeStruct

    band = struct((2 * half * half + 1, func_count, depth), bf16)

    def split(kernel, *operands):
        return pl.pallas_call(
            functools.partial(kernel, half),
            out_shape=(band,) * 2,
            in_specs=[VMEM] * len(operands),
            out_specs=(VMEM,) * 2,
            compiler_params=params(),
            cost_estimate=pl.CostEstimate(flops=0, transcendentals=0, bytes_accessed=2 << 20),
        )(*operands)

    own_x = split(split_x_kernel, own_funcs, potential)
    from_x = (shifted(own_x[1], "brick", 1), shifted(own_x[0], "brick", -1))
    own_y = split(split_y_kernel, *own_x, potential)
    from_y = (shifted(own_y[1], "narrow", 1), shifted(own_y[0], "narrow", -1))
    kernel_store, *_ = lax.optimization_barrier((kernel_store, *own_y))
    kernel_out = pl.pallas_call(
        pair_kernel,
        out_shape=struct((device_count, slot_cap, row_width), bf16),
        in_specs=[VMEM],
        out_specs=VMEM,
        compiler_params=params(),
        cost_estimate=pl.CostEstimate(flops=0, transcendentals=0, bytes_accessed=1 << 20),
    )(kernel_store)
    kernel_in = lax.all_to_all(
        kernel_out, ("brick", "narrow"), split_axis=0, concat_axis=0, tiled=True
    )

    count = half * half
    bands = lax.optimization_barrier((*from_x, *own_y, kernel_out))[:2]
    corners = [bands[sx][: count + 1] if sy else bands[sx][count:] for sx, sy in SIDES]
    from_xy = [shifted(c, "narrow", -1 if sy else 1) for c, (sx, sy) in zip(corners, SIDES)]

    boxes = (*own_x, *bands, *from_y, *from_xy)
    anywhere = pl.BlockSpec(memory_space=pltpu.HBM)
    cells = ext_x * ext_y * depth
    lines = 2 * slot_cap * (row_width // depth + 1)
    outgoing = pl.pallas_call(
        functools.partial(pairs_kernel, half, slot_cap),
        out_shape=struct((device_count, lines, depth), jnp.int16),
        in_specs=[SMEM] + [VMEM] * 11,
        out_specs=VMEM,
        scratch_shapes=[
            pltpu.VMEM((device_count, lines, depth), jnp.float32),
            pltpu.VMEM((pl.cdiv(9 * func_count, depth), 2 * func_count, depth), jnp.float32),
            pltpu.SMEM((device_count,), jnp.int32),
        ],
        compiler_params=params(60),
        cost_estimate=pl.CostEstimate(
            flops=16 * func_count * func_count * cells, transcendentals=0, bytes_accessed=7 << 20
        ),
    )(owner_col, potential, *boxes)
    blocks = lax.all_to_all(outgoing, ("brick", "narrow"), split_axis=0, concat_axis=0, tiled=True)
    steps = 8
    chunk = device_count // steps
    blocks = pl.pallas_call(
        functools.partial(unpack_kernel, slot_cap),
        grid=(steps,),
        out_shape=struct((slot_count, 2, row_width), jnp.float32),
        in_specs=[pl.BlockSpec((chunk, lines, depth), lambda i: (i, 0, 0))],
        out_specs=pl.BlockSpec((chunk * slot_cap, 2, row_width), lambda i: (i, 0, 0)),
        compiler_params=params(),
    )(blocks)

    gradient = pl.pallas_call(
        functools.partial(mix_kernel, half),
        out_shape=struct((atoms, 2, ext_x, ext_y, depth), bf16),
        in_specs=[SMEM, VMEM, VMEM] + [anywhere] * 10,
        out_specs=VMEM,
        scratch_shapes=[
            pltpu.VMEM((atoms, row_width), jnp.float32),
            pltpu.VMEM((ext_x, ext_y, func_count, depth), jnp.float32),
            pltpu.SMEM((device_count,), jnp.int32),
            pltpu.SemaphoreType.DMA((10,)),
        ]
        + [pltpu.VMEM(box.shape, box.dtype) for box in boxes],
        compiler_params=params(60),
        cost_estimate=pl.CostEstimate(
            flops=8 * func_count * func_count * cells, transcendentals=0, bytes_accessed=7 << 20
        ),
    )(owner_col, kernel_in, potential, *boxes)
    return (blocks, gradient.reshape(functions.shape))


def solution(mesh):
    in_specs = (
        P("brick", "narrow", None),
        P("brick", "narrow", None, None, None, None),
        P(("brick", "narrow"), None),
        P(("brick", "narrow"), None),
    )
    out_specs = (P(("brick", "narrow"), None, None), P("brick", "narrow", None, None, None, None))
    return jax.shard_map(body, mesh=mesh, in_specs=in_specs, out_specs=out_specs, check_vma=False)
```

```python
import functools

import jax
import jax.numpy as jnp
from jax import lax
from jax.experimental import pallas as pl
from jax.experimental.pallas import tpu as pltpu
from jax.sharding import Mesh
from jax.sharding import PartitionSpec as P

AT_X = {1: 1, 0: 2}
AT_Y = {1: 3, 0: 4}
AT_XY = {(1, 1): 5, (1, 0): 6, (0, 1): 7, (0, 0): 8}
SIDES = ((0, 0), (0, 1), (1, 0), (1, 1))
STEPS = 64.0
TOP = 32700.0
SMALLEST = 1e-33
VMEM = pl.BlockSpec(memory_space=pltpu.VMEM)
SMEM = pl.BlockSpec(memory_space=pltpu.SMEM)


BRICK, NARROW = ("z", "y"), ("x", "core")
ORDER = ("core", "x", "y", "z")


def place(device, sizes):
    z_bits, y_bits, x_bits, core_bits = (size.bit_length() - 1 for size in sizes)
    core = device & (sizes[3] - 1)
    x = (device >> core_bits) & (sizes[2] - 1)
    y = (device >> (core_bits + x_bits)) & (sizes[1] - 1)
    z = device >> (core_bits + x_bits + y_bits)
    return (((((core << x_bits) + x) << y_bits) + y) << z_bits) + z


def shifted(shard, axis, by):
    size = lax.axis_size(axis)
    return lax.ppermute(shard, axis, [(i, (i + by) % size) for i in range(size)])


def params(mib=16):
    return pltpu.CompilerParams(vmem_limit_bytes=mib << 20)


def packed_rows(rows, func_count):
    value = jnp.concatenate(rows, axis=0)
    pieces = []
    for _ in range(3):
        piece = value.astype(jnp.bfloat16).astype(jnp.float32)
        pieces.append(piece)
        value = value - piece
    count = func_count - 3 * len(rows)
    pieces.append(jnp.zeros((count, value.shape[1]), jnp.float32))
    return jnp.concatenate(pieces, axis=0).astype(jnp.bfloat16)


def unpacked_rows(block, count):
    block = block.astype(jnp.float32)
    return block[:count] + block[count : 2 * count] + block[2 * count : 3 * count]


def split_x_kernel(half, f_ref, pot_ref, *out_refs):
    count = half * half
    func_count = f_ref.shape[0]
    inner = pot_ref.shape[0]
    margin = half - inner // 2
    for x in range(2 * half):
        rows = jnp.swapaxes(f_ref[:, x], 0, 1)
        side, at = divmod(x, half)
        for y in (0, 1):
            start = y * (count + 1) + at * half
            out_refs[side][start : start + half] = rows[y * half : (y + 1) * half]
    for side in (0, 1):
        first = side * (inner - margin)
        out_refs[side][count] = packed_rows(
            [pot_ref[first + i, j : j + 1] for i in range(margin) for j in range(inner)], func_count
        )


def split_y_kernel(half, x0_ref, x1_ref, pot_ref, *out_refs):
    count = half * half
    func_count = x0_ref.shape[1]
    inner = pot_ref.shape[0]
    margin = half - inner // 2
    for side in (0, 1):
        for side_x, x_ref in enumerate((x0_ref, x1_ref)):
            start, taken = side_x * (count + 1), side * (count + 1)
            out_refs[side][start : start + count] = x_ref[taken : taken + count]
        first = side * (inner - margin)
        out_refs[side][count] = packed_rows(
            [pot_ref[i, first + j : first + j + 1] for i in range(inner) for j in range(margin)], func_count
        )


class Boxes:
    def __init__(self, half, refs, pot_ref):
        self.half, self.count = half, half * half
        self.own, self.x, self.y, self.xy = refs[0:2], refs[2:4], refs[4:6], dict(zip(SIDES, refs[6:10]))
        self.pot = pot_ref
        self.inner = pot_ref.shape[0]
        self.margin = half - self.inner // 2
        self.edge = {}

    def columns(self, sides, at_x, at_y):
        side_x, side_y = sides
        at = at_x * self.half + at_y
        return [
            self.own[side_x][side_y * (self.count + 1) + at],
            self.x[side_x][side_y * (self.count + 1) + at],
            self.y[side_y][side_x * (self.count + 1) + at],
            self.xy[sides][1 - side_y + at],
        ]

    def edge_row(self, key, row):
        if key not in self.edge:
            ref = self.xy[key] if isinstance(key, tuple) and key in self.xy else getattr(self, key[0])[key[1]]
            at = self.count
            if key in self.xy:
                at = self.count * key[1]
            self.edge[key] = unpacked_rows(ref[at], self.margin * self.inner)
        return self.edge[key][row : row + 1]

    def potential(self, x, y):
        inner, margin = self.inner, self.margin
        in_x, in_y = (margin <= v < margin + inner for v in (x, y))
        side_x, side_y = x // self.half, y // self.half
        near_x, near_y = x - side_x * (margin + inner), y - side_y * (margin + inner)
        if in_x and in_y:
            return self.pot[x - margin, y - margin : y - margin + 1]
        if in_y:
            return self.edge_row(("x", side_x), near_x * inner + y - margin)
        if in_x:
            return self.edge_row(("y", side_y), (x - margin) * margin + near_y)
        column = near_y if side_y else inner - margin + near_y
        return self.edge_row((side_x, side_y), near_x * inner + column)


def pair_kernel(sizes, k_ref, o_ref):
    z_size, y_size, x_size, core_size = sizes
    rows = k_ref[...].reshape(*sizes, *o_ref.shape[1:])
    for core in range(core_size):
        for x in range(x_size):
            for y in range(y_size):
                at = ((core * x_size + x) * y_size + y) * z_size
                o_ref[at : at + z_size] = rows[:, y, x, core]


def stencil(cell, potential_row, half, x, y, zero_low, zero_high):
    value = cell(x, y)
    beside = jnp.where(zero_high, 0.0, pltpu.roll(value, value.shape[1] - 1, 1)) + jnp.where(
        zero_low, 0.0, pltpu.roll(value, 1, 1)
    )
    for near_x, near_y in ((x + 1, y), (x - 1, y), (x, y + 1), (x, y - 1)):
        if 0 <= near_x < 2 * half and 0 <= near_y < 2 * half:
            beside = beside + cell(near_x, near_y)
    return (3.0 + potential_row(x, y)) * value - 0.5 * beside


def edges(func_count, depth):
    lane = lax.broadcasted_iota(jnp.int32, (func_count, depth), 1)
    return lane == 0, lane == depth - 1


def ranks(owner_ref, count_ref, sizes):
    def clear(i, carry):
        count_ref[owner_ref[i]] = 0
        return carry

    lax.fori_loop(0, owner_ref.shape[0], clear, 0)
    found = []
    for a in range(owner_ref.shape[0]):
        owner = owner_ref[a]
        rank = count_ref[owner]
        count_ref[owner] = rank + 1
        found.append((place(owner, sizes), rank))
    return found


def pairs_kernel(half, cap, sizes, owner_ref, pot_ref, *refs):
    out_ref, wide_ref, sums_ref, count_ref = refs[10:14]
    boxes = Boxes(half, refs[0:10], pot_ref)
    func_count, depth = refs[0].shape[-2:]
    atoms = owner_ref.shape[0]
    low_edge, high_edge = edges(func_count, depth)

    def cell(x, y):
        side_x, at_x = divmod(x, half)
        side_y, at_y = divmod(y, half)
        return boxes.columns((side_x, side_y), at_x, at_y)[0].astype(jnp.float32)

    wide_ref[...] = jnp.zeros(wide_ref.shape, wide_ref.dtype)
    block = {}
    for side_x, side_y in SIDES:
        total = jnp.zeros((2 * func_count, 4 * func_count), jnp.float32)
        for at_x in range(half):
            left, right = [], []
            for at_y in range(half):
                columns = boxes.columns((side_x, side_y), at_x, at_y)
                applied = stencil(
                    cell, boxes.potential, half, side_x * half + at_x, side_y * half + at_y, low_edge, high_edge
                ).astype(jnp.bfloat16)
                left.append(jnp.concatenate([columns[0], applied], axis=0))
                right.append(jnp.concatenate(columns, axis=0))
            total = total + lax.dot_general(
                jnp.concatenate(left, axis=1),
                jnp.concatenate(right, axis=1),
                (((1,), (1,)), ((), ())),
                preferred_element_type=jnp.float32,
            )
        block[side_x, side_y] = total

    def summed(part, *sides):
        return functools.reduce(
            jnp.add, [block[s][:, part * func_count : (part + 1) * func_count] for s in sides]
        )

    parts = [summed(0, *SIDES)] + [None] * 8
    for side in (0, 1):
        parts[AT_X[side]] = summed(1, (side, 0), (side, 1))
        parts[AT_Y[side]] = summed(2, (0, side), (1, side))
    for sides in SIDES:
        parts[AT_XY[sides]] = summed(3, sides)
    width = 9 * func_count
    volume = 1.0 / (4 * half * half * depth)
    sums = jnp.concatenate(parts, axis=1) * volume
    for t in range(0, width, depth):
        sums_ref[t // depth, :, : min(depth, width - t)] = sums[:, t : t + depth]

    def atom_rows(start):
        picked = []
        for i in (0, 1):
            tiles = [sums_ref[t, pl.ds(start + i, atoms, stride=2), :] for t in range(sums_ref.shape[0])]
            picked.append(jnp.concatenate(tiles, axis=1)[:, :width])
        return jnp.concatenate(picked, axis=1)

    coded = []
    for start in (0, func_count):
        row = atom_rows(start)
        largest = jnp.maximum(jnp.max(jnp.abs(row), axis=1, keepdims=True), SMALLEST)
        power = jnp.ceil(STEPS * jnp.log2(largest))
        coded.append((row * (TOP * jnp.exp2(-power / STEPS)), jnp.broadcast_to(power, (atoms, depth))))
    tiles = 2 * width // depth
    for a, (owner, rank) in enumerate(ranks(owner_ref, count_ref, sizes)):
        for m, (row, power) in enumerate(coded):
            for t in range(tiles):
                wide_ref[owner, pl.ds(rank * (2 * tiles) + 2 * t + m, 1), :] = row[
                    a : a + 1, t * depth : (t + 1) * depth
                ]
            wide_ref[owner, pl.ds(cap * 2 * tiles + 2 * rank + m, 1), :] = power[a : a + 1]
    for owner in range(out_ref.shape[0]):
        out_ref[owner] = jnp.round(wide_ref[owner]).astype(jnp.int32).astype(jnp.int16)


def unpack_kernel(cap, sizes, in_ref, out_ref):
    chunks = out_ref.shape[0] // cap
    _, rows, depth = in_ref.shape
    data = rows - 2 * cap
    line = lax.broadcasted_iota(jnp.int32, (data, depth), 0)
    even = line % 2 == 0
    for c in range(chunks):
        at = place(c, sizes) + pl.program_id(0) * (chunks * sizes[0] // in_ref.shape[0])
        values = in_ref[at].astype(jnp.int32).astype(jnp.float32)
        scale = jnp.exp2(values[data:] * (1.0 / STEPS)) * (1.0 / TOP)
        spread = jnp.where(even, scale[0:1], scale[1:2])
        for rank in range(1, cap):
            spread = jnp.where(
                line >= rank * (data // cap),
                jnp.where(even, scale[2 * rank : 2 * rank + 1], scale[2 * rank + 1 : 2 * rank + 2]),
                spread,
            )
        values = values[:data] * spread
        for rank in range(cap):
            for t in range(data // (2 * cap)):
                start = rank * (data // cap) + 2 * t
                out_ref[c * cap + rank, :, t * depth : (t + 1) * depth] = values[start : start + 2]


def mix_kernel(half, sizes, owner_ref, kernel_ref, pot_ref, *refs):
    out_ref, rows_ref, mixed_ref, count_ref, sems = refs[10:15]
    held = refs[15:25]
    copies = [pltpu.make_async_copy(refs[i], held[i], sems.at[i]) for i in range(10)]
    for copy in copies:
        copy.start()
    boxes = Boxes(half, held, pot_ref)
    func_count, depth = refs[0].shape[-2:]
    atoms = owner_ref.shape[0]
    low_edge, high_edge = edges(func_count, depth)
    for a, (owner, rank) in enumerate(ranks(owner_ref, count_ref, sizes)):
        both = kernel_ref[owner].astype(jnp.float32)
        rows_ref[a : a + 1, :] = jnp.where(rank == 0, both[0:1], both[1:2])
    width = 9 * func_count
    matrix = jnp.concatenate([rows_ref[:, :width], rows_ref[:, width:]], axis=0)
    for copy in copies:
        copy.wait()
    for side_x, side_y in SIDES:
        at = (0, AT_X[side_x], AT_Y[side_y], AT_XY[side_x, side_y])
        left = jnp.concatenate(
            [matrix[:, k * func_count : (k + 1) * func_count] for k in at], axis=1
        ).astype(jnp.bfloat16)
        for at_x in range(half):
            for at_y in range(0, half, 2):
                right = jnp.concatenate(
                    [
                        jnp.concatenate(boxes.columns((side_x, side_y), at_x, y), axis=0)
                        for y in (at_y, at_y + 1)
                    ],
                    axis=1,
                )
                got = jnp.dot(left, right, preferred_element_type=jnp.float32)
                for i in (0, 1):
                    mixed_ref[side_x * half + at_x, side_y * half + at_y + i] = got[
                        :, i * depth : (i + 1) * depth
                    ]

    def cell(x, y):
        return mixed_ref[x, y]

    for x in range(2 * half):
        made = [
            stencil(cell, boxes.potential, half, x, y, low_edge, high_edge) for y in range(2 * half)
        ]
        for odd in (0, 1):
            stacked = jnp.stack([m[odd * atoms : (odd + 1) * atoms] for m in made], axis=0)
            out_ref[:, odd, x] = jnp.swapaxes(stacked, 0, 1).astype(out_ref.dtype)


def body(sizes, potential, functions, kernel_store, owners):
    own_funcs = functions[0, 0]
    func_count, ext_x, ext_y, depth = own_funcs.shape
    half = ext_x // 2
    margin = (ext_x - potential.shape[0]) // 2
    device_count = sizes[0] * sizes[1] * sizes[2] * sizes[3]
    owner_col = owners[:, 0]
    atoms = owner_col.shape[0]
    slot_count, row_width = kernel_store.shape
    slot_cap = slot_count // device_count
    bf16 = jnp.bfloat16
    struct = jax.ShapeDtypeStruct

    band = struct((2 * half * half + 1, func_count, depth), bf16)

    def split(kernel, *operands):
        return pl.pallas_call(
            functools.partial(kernel, half),
            out_shape=(band,) * 2,
            in_specs=[VMEM] * len(operands),
            out_specs=(VMEM,) * 2,
            compiler_params=params(),
            cost_estimate=pl.CostEstimate(flops=0, transcendentals=0, bytes_accessed=2 << 20),
        )(*operands)

    own_x = split(split_x_kernel, own_funcs, potential)
    from_x = (shifted(own_x[1], BRICK, 1), shifted(own_x[0], BRICK, -1))
    own_y = split(split_y_kernel, *own_x, potential)
    from_y = (shifted(own_y[1], NARROW, 1), shifted(own_y[0], NARROW, -1))
    kernel_store, *_ = lax.optimization_barrier((kernel_store, *own_y))
    kernel_out = pl.pallas_call(
        functools.partial(pair_kernel, sizes),
        out_shape=struct((device_count, slot_cap, row_width), bf16),
        in_specs=[VMEM],
        out_specs=VMEM,
        compiler_params=params(),
        cost_estimate=pl.CostEstimate(flops=0, transcendentals=0, bytes_accessed=1 << 20),
    )(kernel_store)
    kernel_in = lax.all_to_all(
        kernel_out, ORDER, split_axis=0, concat_axis=0, tiled=True
    )

    count = half * half
    bands = lax.optimization_barrier((*from_x, *own_y, kernel_out))[:2]
    corners = [bands[sx][: count + 1] if sy else bands[sx][count:] for sx, sy in SIDES]
    from_xy = [shifted(c, NARROW, -1 if sy else 1) for c, (sx, sy) in zip(corners, SIDES)]

    boxes = (*own_x, *bands, *from_y, *from_xy)
    anywhere = pl.BlockSpec(memory_space=pltpu.HBM)
    cells = ext_x * ext_y * depth
    lines = 2 * slot_cap * (row_width // depth + 1)
    outgoing = pl.pallas_call(
        functools.partial(pairs_kernel, half, slot_cap, sizes),
        out_shape=struct((device_count, lines, depth), jnp.int16),
        in_specs=[SMEM] + [VMEM] * 11,
        out_specs=VMEM,
        scratch_shapes=[
            pltpu.VMEM((device_count, lines, depth), jnp.float32),
            pltpu.VMEM((pl.cdiv(9 * func_count, depth), 2 * func_count, depth), jnp.float32),
            pltpu.SMEM((device_count,), jnp.int32),
        ],
        compiler_params=params(60),
        cost_estimate=pl.CostEstimate(
            flops=16 * func_count * func_count * cells, transcendentals=0, bytes_accessed=7 << 20
        ),
    )(owner_col, potential, *boxes)
    blocks = lax.all_to_all(outgoing, ORDER, split_axis=0, concat_axis=0, tiled=True)
    steps = 2
    chunk = device_count // steps
    blocks = pl.pallas_call(
        functools.partial(unpack_kernel, slot_cap, sizes),
        grid=(steps,),
        out_shape=struct((slot_count, 2, row_width), jnp.float32),
        in_specs=[VMEM],
        out_specs=pl.BlockSpec((chunk * slot_cap, 2, row_width), lambda i: (i, 0, 0)),
        compiler_params=params(),
    )(blocks)

    gradient = pl.pallas_call(
        functools.partial(mix_kernel, half, sizes),
        out_shape=struct((atoms, 2, ext_x, ext_y, depth), bf16),
        in_specs=[SMEM, VMEM, VMEM] + [anywhere] * 10,
        out_specs=VMEM,
        scratch_shapes=[
            pltpu.VMEM((atoms, row_width), jnp.float32),
            pltpu.VMEM((ext_x, ext_y, func_count, depth), jnp.float32),
            pltpu.SMEM((device_count,), jnp.int32),
            pltpu.SemaphoreType.DMA((10,)),
        ]
        + [pltpu.VMEM(box.shape, box.dtype) for box in boxes],
        compiler_params=params(60),
        cost_estimate=pl.CostEstimate(
            flops=8 * func_count * func_count * cells, transcendentals=0, bytes_accessed=7 << 20
        ),
    )(owner_col, kernel_in, potential, *boxes)
    return (blocks, gradient.reshape(functions.shape))


def solution(mesh):
    sizes = (mesh.shape["brick"] // 4, 4, mesh.shape["narrow"] // 2, 2)
    mesh = Mesh(mesh.devices.reshape(sizes), BRICK + NARROW)
    every = BRICK + NARROW
    in_specs = (P(BRICK, NARROW, None), P(BRICK, NARROW, None, None, None, None), P(every, None), P(every, None))
    out_specs = (P(every, None, None), P(BRICK, NARROW, None, None, None, None))
    return jax.shard_map(
        functools.partial(body, sizes), mesh=mesh, in_specs=in_specs, out_specs=out_specs, check_vma=False
    )
```

```python
import functools

import jax
import jax.numpy as jnp
from jax import lax
from jax.experimental import pallas as pl
from jax.experimental.pallas import tpu as pltpu
from jax.sharding import Mesh
from jax.sharding import PartitionSpec as P

AT_X = {1: 1, 0: 2}
AT_Y = {1: 3, 0: 4}
AT_XY = {(1, 1): 5, (1, 0): 6, (0, 1): 7, (0, 0): 8}
SIDES = ((0, 0), (0, 1), (1, 0), (1, 1))
STEPS = 64.0
TOP = 32700.0
SMALLEST = 1e-33
VMEM = pl.BlockSpec(memory_space=pltpu.VMEM)
SMEM = pl.BlockSpec(memory_space=pltpu.SMEM)


BRICK, NARROW = ("z", "y"), ("x", "core")
ORDER = ("core", "x", "y", "z")
ROWS_ORDER = ("y", "core", "x", "z")


def place(device, sizes):
    z_bits, y_bits, x_bits, core_bits = (size.bit_length() - 1 for size in sizes)
    core = device & (sizes[3] - 1)
    x = (device >> core_bits) & (sizes[2] - 1)
    y = (device >> (core_bits + x_bits)) & (sizes[1] - 1)
    z = device >> (core_bits + x_bits + y_bits)
    return (((((core << x_bits) + x) << y_bits) + y) << z_bits) + z


def rows_place(device, sizes):
    z_bits, y_bits, x_bits, core_bits = (size.bit_length() - 1 for size in sizes)
    core = device & (sizes[3] - 1)
    x = (device >> core_bits) & (sizes[2] - 1)
    y = (device >> (core_bits + x_bits)) & (sizes[1] - 1)
    z = device >> (core_bits + x_bits + y_bits)
    return (((((y << core_bits) + core) << x_bits) + x) << z_bits) + z


def shifted(shard, axis, by):
    size = lax.axis_size(axis)
    return lax.ppermute(shard, axis, [(i, (i + by) % size) for i in range(size)])


def params(mib=16):
    return pltpu.CompilerParams(vmem_limit_bytes=mib << 20)


def packed_rows(rows, func_count):
    value = jnp.concatenate(rows, axis=0)
    pieces = []
    for _ in range(3):
        piece = value.astype(jnp.bfloat16).astype(jnp.float32)
        pieces.append(piece)
        value = value - piece
    count = func_count - 3 * len(rows)
    pieces.append(jnp.zeros((count, value.shape[1]), jnp.float32))
    return jnp.concatenate(pieces, axis=0).astype(jnp.bfloat16)


def unpacked_rows(block, count):
    block = block.astype(jnp.float32)
    return block[:count] + block[count : 2 * count] + block[2 * count : 3 * count]


def split_x_kernel(half, f_ref, pot_ref, *out_refs):
    count = half * half
    func_count = f_ref.shape[0]
    inner = pot_ref.shape[0]
    margin = half - inner // 2
    for x in range(2 * half):
        rows = jnp.swapaxes(f_ref[:, x], 0, 1)
        side, at = divmod(x, half)
        for y in (0, 1):
            start = y * (count + 1) + at * half
            out_refs[side][start : start + half] = rows[y * half : (y + 1) * half]
    for side in (0, 1):
        first = side * (inner - margin)
        out_refs[side][count] = packed_rows(
            [pot_ref[first + i, j : j + 1] for i in range(margin) for j in range(inner)], func_count
        )


def split_y_kernel(half, x0_ref, x1_ref, pot_ref, *out_refs):
    count = half * half
    func_count = x0_ref.shape[1]
    inner = pot_ref.shape[0]
    margin = half - inner // 2
    for side in (0, 1):
        for side_x, x_ref in enumerate((x0_ref, x1_ref)):
            start, taken = side_x * (count + 1), side * (count + 1)
            out_refs[side][start : start + count] = x_ref[taken : taken + count]
        first = side * (inner - margin)
        out_refs[side][count] = packed_rows(
            [pot_ref[i, first + j : first + j + 1] for i in range(inner) for j in range(margin)], func_count
        )


class Boxes:
    def __init__(self, half, refs, pot_ref):
        self.half, self.count = half, half * half
        self.own, self.x, self.y, self.xy = refs[0:2], refs[2:4], refs[4:6], dict(zip(SIDES, refs[6:10]))
        self.pot = pot_ref
        self.inner = pot_ref.shape[0]
        self.margin = half - self.inner // 2
        self.edge = {}

    def columns(self, sides, at_x, at_y):
        side_x, side_y = sides
        at = at_x * self.half + at_y
        return [
            self.own[side_x][side_y * (self.count + 1) + at],
            self.x[side_x][side_y * (self.count + 1) + at],
            self.y[side_y][side_x * (self.count + 1) + at],
            self.xy[sides][1 - side_y + at],
        ]

    def edge_row(self, key, row):
        if key not in self.edge:
            ref = self.xy[key] if isinstance(key, tuple) and key in self.xy else getattr(self, key[0])[key[1]]
            at = self.count
            if key in self.xy:
                at = self.count * key[1]
            self.edge[key] = unpacked_rows(ref[at], self.margin * self.inner)
        return self.edge[key][row : row + 1]

    def potential(self, x, y):
        inner, margin = self.inner, self.margin
        in_x, in_y = (margin <= v < margin + inner for v in (x, y))
        side_x, side_y = x // self.half, y // self.half
        near_x, near_y = x - side_x * (margin + inner), y - side_y * (margin + inner)
        if in_x and in_y:
            return self.pot[x - margin, y - margin : y - margin + 1]
        if in_y:
            return self.edge_row(("x", side_x), near_x * inner + y - margin)
        if in_x:
            return self.edge_row(("y", side_y), (x - margin) * margin + near_y)
        column = near_y if side_y else inner - margin + near_y
        return self.edge_row((side_x, side_y), near_x * inner + column)


def pair_kernel(sizes, k_ref, o_ref):
    z_size, y_size, x_size, core_size = sizes
    rows = k_ref[...].reshape(*sizes, *o_ref.shape[1:])
    for core in range(core_size):
        for x in range(x_size):
            for y in range(y_size):
                at = ((y * core_size + core) * x_size + x) * z_size
                o_ref[at : at + z_size] = rows[:, y, x, core]


def stencil(cell, potential_row, half, x, y, zero_low, zero_high):
    value = cell(x, y)
    beside = jnp.where(zero_high, 0.0, pltpu.roll(value, value.shape[1] - 1, 1)) + jnp.where(
        zero_low, 0.0, pltpu.roll(value, 1, 1)
    )
    for near_x, near_y in ((x + 1, y), (x - 1, y), (x, y + 1), (x, y - 1)):
        if 0 <= near_x < 2 * half and 0 <= near_y < 2 * half:
            beside = beside + cell(near_x, near_y)
    return (3.0 + potential_row(x, y)) * value - 0.5 * beside


def edges(func_count, depth):
    lane = lax.broadcasted_iota(jnp.int32, (func_count, depth), 1)
    return lane == 0, lane == depth - 1


def ranks(owner_ref, count_ref):
    def clear(i, carry):
        count_ref[owner_ref[i]] = 0
        return carry

    lax.fori_loop(0, owner_ref.shape[0], clear, 0)
    found = []
    for a in range(owner_ref.shape[0]):
        owner = owner_ref[a]
        rank = count_ref[owner]
        count_ref[owner] = rank + 1
        found.append((owner, rank))
    return found


def pairs_kernel(half, cap, sizes, owner_ref, pot_ref, *refs):
    out_ref, wide_ref, sums_ref, count_ref = refs[10:14]
    boxes = Boxes(half, refs[0:10], pot_ref)
    func_count, depth = refs[0].shape[-2:]
    atoms = owner_ref.shape[0]
    low_edge, high_edge = edges(func_count, depth)

    def cell(x, y):
        side_x, at_x = divmod(x, half)
        side_y, at_y = divmod(y, half)
        return boxes.columns((side_x, side_y), at_x, at_y)[0].astype(jnp.float32)

    wide_ref[...] = jnp.zeros(wide_ref.shape, wide_ref.dtype)
    block = {}
    for side_x, side_y in SIDES:
        total = jnp.zeros((2 * func_count, 4 * func_count), jnp.float32)
        for at_x in range(half):
            left, right = [], []
            for at_y in range(half):
                columns = boxes.columns((side_x, side_y), at_x, at_y)
                applied = stencil(
                    cell, boxes.potential, half, side_x * half + at_x, side_y * half + at_y, low_edge, high_edge
                ).astype(jnp.bfloat16)
                left.append(jnp.concatenate([columns[0], applied], axis=0))
                right.append(jnp.concatenate(columns, axis=0))
            total = total + lax.dot_general(
                jnp.concatenate(left, axis=1),
                jnp.concatenate(right, axis=1),
                (((1,), (1,)), ((), ())),
                preferred_element_type=jnp.float32,
            )
        block[side_x, side_y] = total

    def summed(part, *sides):
        return functools.reduce(
            jnp.add, [block[s][:, part * func_count : (part + 1) * func_count] for s in sides]
        )

    parts = [summed(0, *SIDES)] + [None] * 8
    for side in (0, 1):
        parts[AT_X[side]] = summed(1, (side, 0), (side, 1))
        parts[AT_Y[side]] = summed(2, (0, side), (1, side))
    for sides in SIDES:
        parts[AT_XY[sides]] = summed(3, sides)
    width = 9 * func_count
    volume = 1.0 / (4 * half * half * depth)
    sums = jnp.concatenate(parts, axis=1) * volume
    for t in range(0, width, depth):
        sums_ref[t // depth, :, : min(depth, width - t)] = sums[:, t : t + depth]

    def atom_rows(start):
        picked = []
        for i in (0, 1):
            tiles = [sums_ref[t, pl.ds(start + i, atoms, stride=2), :] for t in range(sums_ref.shape[0])]
            picked.append(jnp.concatenate(tiles, axis=1)[:, :width])
        return jnp.concatenate(picked, axis=1)

    coded = []
    for start in (0, func_count):
        row = atom_rows(start)
        largest = jnp.maximum(jnp.max(jnp.abs(row), axis=1, keepdims=True), SMALLEST)
        power = jnp.ceil(STEPS * jnp.log2(largest))
        coded.append((row * (TOP * jnp.exp2(-power / STEPS)), jnp.broadcast_to(power, (atoms, depth))))
    tiles = 2 * width // depth
    for a, (owner, rank) in enumerate(ranks(owner_ref, count_ref)):
        at = place(owner, sizes)
        for m, (row, power) in enumerate(coded):
            for t in range(tiles):
                wide_ref[at, pl.ds(rank * (2 * tiles) + 2 * t + m, 1), :] = row[
                    a : a + 1, t * depth : (t + 1) * depth
                ]
            wide_ref[at, pl.ds(cap * 2 * tiles + 2 * rank + m, 1), :] = power[a : a + 1]
    for owner in range(out_ref.shape[0]):
        out_ref[owner] = jnp.round(wide_ref[owner]).astype(jnp.int32).astype(jnp.int16)


def unpack_kernel(cap, sizes, in_ref, out_ref):
    chunks = out_ref.shape[0] // cap
    _, rows, depth = in_ref.shape
    data = rows - 2 * cap
    line = lax.broadcasted_iota(jnp.int32, (data, depth), 0)
    even = line % 2 == 0
    for c in range(chunks):
        at = place(c, sizes) + pl.program_id(0) * (chunks * sizes[0] // in_ref.shape[0])
        values = in_ref[at].astype(jnp.int32).astype(jnp.float32)
        scale = jnp.exp2(values[data:] * (1.0 / STEPS)) * (1.0 / TOP)
        spread = jnp.where(even, scale[0:1], scale[1:2])
        for rank in range(1, cap):
            spread = jnp.where(
                line >= rank * (data // cap),
                jnp.where(even, scale[2 * rank : 2 * rank + 1], scale[2 * rank + 1 : 2 * rank + 2]),
                spread,
            )
        values = values[:data] * spread
        for rank in range(cap):
            for t in range(data // (2 * cap)):
                start = rank * (data // cap) + 2 * t
                out_ref[c * cap + rank, :, t * depth : (t + 1) * depth] = values[start : start + 2]


def keep_kernel(*refs):
    number = len(refs) // 2
    for given, kept in zip(refs[:number], refs[number:]):
        kept[...] = given[...]


def mix_kernel(half, sizes, owner_ref, kernel_ref, pot_ref, *refs):
    out_ref, rows_ref, mixed_ref, count_ref, sems = refs[10:15]
    held = refs[15:25]
    copies = [pltpu.make_async_copy(refs[i], held[i], sems.at[i]) for i in range(10)]
    for copy in copies:
        copy.start()
    boxes = Boxes(half, held, pot_ref)
    func_count, depth = refs[0].shape[-2:]
    atoms = owner_ref.shape[0]
    low_edge, high_edge = edges(func_count, depth)
    for a, (owner, rank) in enumerate(ranks(owner_ref, count_ref)):
        both = kernel_ref[rows_place(owner, sizes)].astype(jnp.float32)
        rows_ref[a : a + 1, :] = jnp.where(rank == 0, both[0:1], both[1:2])
    width = 9 * func_count
    matrix = jnp.concatenate([rows_ref[:, :width], rows_ref[:, width:]], axis=0)
    for copy in copies:
        copy.wait()
    for side_x, side_y in SIDES:
        at = (0, AT_X[side_x], AT_Y[side_y], AT_XY[side_x, side_y])
        left = jnp.concatenate(
            [matrix[:, k * func_count : (k + 1) * func_count] for k in at], axis=1
        ).astype(jnp.bfloat16)
        for at_x in range(half):
            for at_y in range(0, half, 2):
                right = jnp.concatenate(
                    [
                        jnp.concatenate(boxes.columns((side_x, side_y), at_x, y), axis=0)
                        for y in (at_y, at_y + 1)
                    ],
                    axis=1,
                )
                got = jnp.dot(left, right, preferred_element_type=jnp.float32)
                for i in (0, 1):
                    mixed_ref[side_x * half + at_x, side_y * half + at_y + i] = got[
                        :, i * depth : (i + 1) * depth
                    ]

    def cell(x, y):
        return mixed_ref[x, y]

    for x in range(2 * half):
        made = [
            stencil(cell, boxes.potential, half, x, y, low_edge, high_edge) for y in range(2 * half)
        ]
        for odd in (0, 1):
            stacked = jnp.stack([m[odd * atoms : (odd + 1) * atoms] for m in made], axis=0)
            out_ref[:, odd, x] = jnp.swapaxes(stacked, 0, 1).astype(out_ref.dtype)


def body(sizes, potential, functions, kernel_store, owners):
    own_funcs = functions[0, 0]
    func_count, ext_x, ext_y, depth = own_funcs.shape
    half = ext_x // 2
    margin = (ext_x - potential.shape[0]) // 2
    device_count = sizes[0] * sizes[1] * sizes[2] * sizes[3]
    owner_col = owners[:, 0]
    atoms = owner_col.shape[0]
    slot_count, row_width = kernel_store.shape
    slot_cap = slot_count // device_count
    bf16 = jnp.bfloat16
    struct = jax.ShapeDtypeStruct

    band = struct((2 * half * half + 1, func_count, depth), bf16)

    def split(kernel, *operands):
        return pl.pallas_call(
            functools.partial(kernel, half),
            out_shape=(band,) * 2,
            in_specs=[VMEM] * len(operands),
            out_specs=(VMEM,) * 2,
            compiler_params=params(),
            cost_estimate=pl.CostEstimate(flops=0, transcendentals=0, bytes_accessed=2 << 20),
        )(*operands)

    own_x = split(split_x_kernel, own_funcs, potential)
    from_x = (shifted(own_x[1], BRICK, 1), shifted(own_x[0], BRICK, -1))
    own_y = split(split_y_kernel, *own_x, potential)
    from_y = (shifted(own_y[1], NARROW, 1), shifted(own_y[0], NARROW, -1))
    kernel_store, *_ = lax.optimization_barrier((kernel_store, *own_y))
    kernel_out = pl.pallas_call(
        functools.partial(pair_kernel, sizes),
        out_shape=struct((device_count, slot_cap, row_width), bf16),
        in_specs=[VMEM],
        out_specs=VMEM,
        compiler_params=params(),
        cost_estimate=pl.CostEstimate(flops=0, transcendentals=0, bytes_accessed=1 << 20),
    )(kernel_store)
    kernel_in = lax.all_to_all(
        kernel_out, ROWS_ORDER, split_axis=0, concat_axis=0, tiled=True
    )

    count = half * half
    bands = lax.optimization_barrier((*from_x, *own_y, kernel_out))[:2]
    corners = [bands[sx][: count + 1] if sy else bands[sx][count:] for sx, sy in SIDES]
    from_xy = [shifted(c, NARROW, -1 if sy else 1) for c, (sx, sy) in zip(corners, SIDES)]

    boxes = (*own_x, *bands, *from_y, *from_xy)
    anywhere = pl.BlockSpec(memory_space=pltpu.HBM)
    cells = ext_x * ext_y * depth
    lines = 2 * slot_cap * (row_width // depth + 1)
    kept = [
        pl.pallas_call(
            keep_kernel,
            out_shape=struct(box.shape, box.dtype),
            in_specs=[VMEM],
            out_specs=VMEM,
            compiler_params=params(24),
            cost_estimate=pl.CostEstimate(flops=0, transcendentals=0, bytes_accessed=1 << 19),
        )(box)
        for box in from_xy
    ]
    owner_first, *kept = lax.optimization_barrier((owner_col, *kept))
    outgoing = pl.pallas_call(
        functools.partial(pairs_kernel, half, slot_cap, sizes),
        out_shape=struct((device_count, lines, depth), jnp.int16),
        in_specs=[SMEM] + [VMEM] * 11,
        out_specs=VMEM,
        scratch_shapes=[
            pltpu.VMEM((device_count, lines, depth), jnp.float32),
            pltpu.VMEM((pl.cdiv(9 * func_count, depth), 2 * func_count, depth), jnp.float32),
            pltpu.SMEM((device_count,), jnp.int32),
        ],
        compiler_params=params(24),
        cost_estimate=pl.CostEstimate(
            flops=16 * func_count * func_count * cells, transcendentals=0, bytes_accessed=7 << 20
        ),
    )(owner_first, potential, *boxes)
    blocks = lax.all_to_all(outgoing, ORDER, split_axis=0, concat_axis=0, tiled=True)
    steps = 2
    chunk = device_count // steps
    blocks = pl.pallas_call(
        functools.partial(unpack_kernel, slot_cap, sizes),
        grid=(steps,),
        out_shape=struct((slot_count, 2, row_width), jnp.float32),
        in_specs=[VMEM],
        out_specs=pl.BlockSpec((chunk * slot_cap, 2, row_width), lambda i: (i, 0, 0)),
        compiler_params=params(),
    )(blocks)

    gradient = pl.pallas_call(
        functools.partial(mix_kernel, half, sizes),
        out_shape=struct((atoms, 2, ext_x, ext_y, depth), bf16),
        in_specs=[SMEM, VMEM, VMEM] + [anywhere] * 10,
        out_specs=VMEM,
        scratch_shapes=[
            pltpu.VMEM((atoms, row_width), jnp.float32),
            pltpu.VMEM((ext_x, ext_y, func_count, depth), jnp.float32),
            pltpu.SMEM((device_count,), jnp.int32),
            pltpu.SemaphoreType.DMA((10,)),
        ]
        + [pltpu.VMEM(box.shape, box.dtype) for box in boxes],
        compiler_params=params(60),
        cost_estimate=pl.CostEstimate(
            flops=8 * func_count * func_count * cells, transcendentals=0, bytes_accessed=7 << 20
        ),
    )(owner_col, kernel_in, potential, *boxes[:6], *kept)
    return (blocks, gradient.reshape(functions.shape))


def solution(mesh):
    sizes = (mesh.shape["brick"] // 4, 4, mesh.shape["narrow"] // 2, 2)
    mesh = Mesh(mesh.devices.reshape(sizes), BRICK + NARROW)
    every = BRICK + NARROW
    in_specs = (P(BRICK, NARROW, None), P(BRICK, NARROW, None, None, None, None), P(every, None), P(every, None))
    out_specs = (P(every, None, None), P(BRICK, NARROW, None, None, None, None))
    return jax.shard_map(
        functools.partial(body, sizes), mesh=mesh, in_specs=in_specs, out_specs=out_specs, check_vma=False
    )
```

```python
import functools

import jax
import jax.numpy as jnp
from jax import lax
from jax.experimental import pallas as pl
from jax.experimental.pallas import tpu as pltpu
from jax.sharding import Mesh
from jax.sharding import PartitionSpec as P

AT_X = {1: 1, 0: 2}
AT_Y = {1: 3, 0: 4}
AT_XY = {(1, 1): 5, (1, 0): 6, (0, 1): 7, (0, 0): 8}
SIDES = ((0, 0), (0, 1), (1, 0), (1, 1))
STEPS = 64.0
TOP = 32700.0
SMALLEST = 1e-33
VMEM = pl.BlockSpec(memory_space=pltpu.VMEM)
SMEM = pl.BlockSpec(memory_space=pltpu.SMEM)


BRICK, NARROW = ("z", "y"), ("x", "core")
ORDER = ("core", "x", "y", "z")
ROWS_ORDER = ("y", "core", "x", "z")


def place(device, sizes):
    z_bits, y_bits, x_bits, core_bits = (size.bit_length() - 1 for size in sizes)
    core = device & (sizes[3] - 1)
    x = (device >> core_bits) & (sizes[2] - 1)
    y = (device >> (core_bits + x_bits)) & (sizes[1] - 1)
    z = device >> (core_bits + x_bits + y_bits)
    return (((((core << x_bits) + x) << y_bits) + y) << z_bits) + z


def rows_place(device, sizes):
    z_bits, y_bits, x_bits, core_bits = (size.bit_length() - 1 for size in sizes)
    core = device & (sizes[3] - 1)
    x = (device >> core_bits) & (sizes[2] - 1)
    y = (device >> (core_bits + x_bits)) & (sizes[1] - 1)
    z = device >> (core_bits + x_bits + y_bits)
    return (((((y << core_bits) + core) << x_bits) + x) << z_bits) + z


def shifted(shard, axis, by):
    size = lax.axis_size(axis)
    return lax.ppermute(shard, axis, [(i, (i + by) % size) for i in range(size)])


def params(mib=16):
    return pltpu.CompilerParams(vmem_limit_bytes=mib << 20)


def packed_rows(rows, func_count):
    value = jnp.concatenate(rows, axis=0)
    pieces = []
    for _ in range(3):
        piece = value.astype(jnp.bfloat16).astype(jnp.float32)
        pieces.append(piece)
        value = value - piece
    count = func_count - 3 * len(rows)
    pieces.append(jnp.zeros((count, value.shape[1]), jnp.float32))
    return jnp.concatenate(pieces, axis=0).astype(jnp.bfloat16)


def unpacked_rows(block, count):
    block = block.astype(jnp.float32)
    return block[:count] + block[count : 2 * count] + block[2 * count : 3 * count]


def split_x_kernel(half, f_ref, pot_ref, *out_refs):
    count = half * half
    func_count = f_ref.shape[0]
    inner = pot_ref.shape[0]
    margin = half - inner // 2
    for x in range(2 * half):
        rows = jnp.swapaxes(f_ref[:, x], 0, 1)
        side, at = divmod(x, half)
        for y in (0, 1):
            start = y * (count + 1) + at * half
            out_refs[side][start : start + half] = rows[y * half : (y + 1) * half]
    for side in (0, 1):
        first = side * (inner - margin)
        out_refs[side][count] = packed_rows(
            [pot_ref[first + i, j : j + 1] for i in range(margin) for j in range(inner)], func_count
        )


def split_y_kernel(half, x0_ref, x1_ref, pot_ref, *out_refs):
    count = half * half
    func_count = x0_ref.shape[1]
    inner = pot_ref.shape[0]
    margin = half - inner // 2
    for side in (0, 1):
        for side_x, x_ref in enumerate((x0_ref, x1_ref)):
            start, taken = side_x * (count + 1), side * (count + 1)
            out_refs[side][start : start + count] = x_ref[taken : taken + count]
        first = side * (inner - margin)
        out_refs[side][count] = packed_rows(
            [pot_ref[i, first + j : first + j + 1] for i in range(inner) for j in range(margin)], func_count
        )


class Boxes:
    def __init__(self, half, refs, pot_ref):
        self.half, self.count = half, half * half
        self.own, self.x, self.y, self.xy = refs[0:2], refs[2:4], refs[4:6], dict(zip(SIDES, refs[6:10]))
        self.pot = pot_ref
        self.inner = pot_ref.shape[0]
        self.margin = half - self.inner // 2
        self.edge = {}

    def columns(self, sides, at_x, at_y):
        side_x, side_y = sides
        at = at_x * self.half + at_y
        return [
            self.own[side_x][side_y * (self.count + 1) + at],
            self.x[side_x][side_y * (self.count + 1) + at],
            self.y[side_y][side_x * (self.count + 1) + at],
            self.xy[sides][1 - side_y + at],
        ]

    def edge_row(self, key, row):
        if key not in self.edge:
            ref = self.xy[key] if isinstance(key, tuple) and key in self.xy else getattr(self, key[0])[key[1]]
            at = self.count
            if key in self.xy:
                at = self.count * key[1]
            self.edge[key] = unpacked_rows(ref[at], self.margin * self.inner)
        return self.edge[key][row : row + 1]

    def potential(self, x, y):
        inner, margin = self.inner, self.margin
        in_x, in_y = (margin <= v < margin + inner for v in (x, y))
        side_x, side_y = x // self.half, y // self.half
        near_x, near_y = x - side_x * (margin + inner), y - side_y * (margin + inner)
        if in_x and in_y:
            return self.pot[x - margin, y - margin : y - margin + 1]
        if in_y:
            return self.edge_row(("x", side_x), near_x * inner + y - margin)
        if in_x:
            return self.edge_row(("y", side_y), (x - margin) * margin + near_y)
        column = near_y if side_y else inner - margin + near_y
        return self.edge_row((side_x, side_y), near_x * inner + column)


def pair_kernel(sizes, k_ref, o_ref):
    z_size, y_size, x_size, core_size = sizes
    rows = k_ref[...].reshape(*sizes, *o_ref.shape[1:])
    for core in range(core_size):
        for x in range(x_size):
            for y in range(y_size):
                at = ((y * core_size + core) * x_size + x) * z_size
                o_ref[at : at + z_size] = rows[:, y, x, core]


def stencil(cell, potential_row, half, x, y, zero_low, zero_high):
    value = cell(x, y)
    beside = jnp.where(zero_high, 0.0, pltpu.roll(value, value.shape[1] - 1, 1)) + jnp.where(
        zero_low, 0.0, pltpu.roll(value, 1, 1)
    )
    for near_x, near_y in ((x + 1, y), (x - 1, y), (x, y + 1), (x, y - 1)):
        if 0 <= near_x < 2 * half and 0 <= near_y < 2 * half:
            beside = beside + cell(near_x, near_y)
    return (3.0 + potential_row(x, y)) * value - 0.5 * beside


def edges(func_count, depth):
    lane = lax.broadcasted_iota(jnp.int32, (func_count, depth), 1)
    return lane == 0, lane == depth - 1


def ranks(owner_ref, count_ref):
    def clear(i, carry):
        count_ref[owner_ref[i]] = 0
        return carry

    lax.fori_loop(0, owner_ref.shape[0], clear, 0)
    found = []
    for a in range(owner_ref.shape[0]):
        owner = owner_ref[a]
        rank = count_ref[owner]
        count_ref[owner] = rank + 1
        found.append((owner, rank))
    return found


def pairs_kernel(half, cap, sizes, owner_ref, pot_ref, *refs):
    out_ref, wide_ref, sums_ref, count_ref = refs[10:14]
    boxes = Boxes(half, refs[0:10], pot_ref)
    func_count, depth = refs[0].shape[-2:]
    atoms = owner_ref.shape[0]
    low_edge, high_edge = edges(func_count, depth)

    def cell(x, y):
        side_x, at_x = divmod(x, half)
        side_y, at_y = divmod(y, half)
        return boxes.columns((side_x, side_y), at_x, at_y)[0].astype(jnp.float32)

    wide_ref[...] = jnp.zeros(wide_ref.shape, wide_ref.dtype)
    block = {}
    for side_x, side_y in SIDES:
        total = jnp.zeros((2 * func_count, 4 * func_count), jnp.float32)
        for at_x in range(half):
            left, right = [], []
            for at_y in range(half):
                columns = boxes.columns((side_x, side_y), at_x, at_y)
                applied = stencil(
                    cell, boxes.potential, half, side_x * half + at_x, side_y * half + at_y, low_edge, high_edge
                ).astype(jnp.bfloat16)
                left.append(jnp.concatenate([columns[0], applied], axis=0))
                right.append(jnp.concatenate(columns, axis=0))
            total = total + lax.dot_general(
                jnp.concatenate(left, axis=1),
                jnp.concatenate(right, axis=1),
                (((1,), (1,)), ((), ())),
                preferred_element_type=jnp.float32,
            )
        block[side_x, side_y] = total

    def summed(part, *sides):
        return functools.reduce(
            jnp.add, [block[s][:, part * func_count : (part + 1) * func_count] for s in sides]
        )

    parts = [summed(0, *SIDES)] + [None] * 8
    for side in (0, 1):
        parts[AT_X[side]] = summed(1, (side, 0), (side, 1))
        parts[AT_Y[side]] = summed(2, (0, side), (1, side))
    for sides in SIDES:
        parts[AT_XY[sides]] = summed(3, sides)
    width = 9 * func_count
    volume = 1.0 / (4 * half * half * depth)
    sums = jnp.concatenate(parts, axis=1) * volume
    for t in range(0, width, depth):
        sums_ref[t // depth, :, : min(depth, width - t)] = sums[:, t : t + depth]

    def atom_rows(start):
        picked = []
        for i in (0, 1):
            tiles = [sums_ref[t, pl.ds(start + i, atoms, stride=2), :] for t in range(sums_ref.shape[0])]
            picked.append(jnp.concatenate(tiles, axis=1)[:, :width])
        return jnp.concatenate(picked, axis=1)

    coded = []
    for start in (0, func_count):
        row = atom_rows(start)
        largest = jnp.maximum(jnp.max(jnp.abs(row), axis=1, keepdims=True), SMALLEST)
        power = jnp.ceil(STEPS * jnp.log2(largest))
        coded.append((row * (TOP * jnp.exp2(-power / STEPS)), jnp.broadcast_to(power, (atoms, depth))))
    tiles = 2 * width // depth
    for a, (owner, rank) in enumerate(ranks(owner_ref, count_ref)):
        at = place(owner, sizes)
        for m, (row, power) in enumerate(coded):
            for t in range(tiles):
                wide_ref[at, pl.ds(rank * (2 * tiles) + 2 * t + m, 1), :] = row[
                    a : a + 1, t * depth : (t + 1) * depth
                ]
            wide_ref[at, pl.ds(cap * 2 * tiles + 2 * rank + m, 1), :] = power[a : a + 1]
    for owner in range(out_ref.shape[0]):
        out_ref[owner] = jnp.round(wide_ref[owner]).astype(jnp.int32).astype(jnp.int16)


def unpack_kernel(cap, sizes, in_ref, out_ref):
    chunks = out_ref.shape[0] // cap
    _, rows, depth = in_ref.shape
    data = rows - 2 * cap
    line = lax.broadcasted_iota(jnp.int32, (data, depth), 0)
    even = line % 2 == 0
    for c in range(chunks):
        at = place(c, sizes) + pl.program_id(0) * (chunks * sizes[0] // in_ref.shape[0])
        values = in_ref[at].astype(jnp.int32).astype(jnp.float32)
        scale = jnp.exp2(values[data:] * (1.0 / STEPS)) * (1.0 / TOP)
        spread = jnp.where(even, scale[0:1], scale[1:2])
        for rank in range(1, cap):
            spread = jnp.where(
                line >= rank * (data // cap),
                jnp.where(even, scale[2 * rank : 2 * rank + 1], scale[2 * rank + 1 : 2 * rank + 2]),
                spread,
            )
        values = values[:data] * spread
        for rank in range(cap):
            for t in range(data // (2 * cap)):
                start = rank * (data // cap) + 2 * t
                out_ref[c * cap + rank, :, t * depth : (t + 1) * depth] = values[start : start + 2]


def mix_kernel(half, sizes, owner_ref, kernel_ref, pot_ref, *refs):
    out_ref, rows_ref, mixed_ref, count_ref, sems = refs[10:15]
    held = refs[15:25]
    copies = [pltpu.make_async_copy(refs[i], held[i], sems.at[i]) for i in range(10)]
    for copy in copies:
        copy.start()
    boxes = Boxes(half, held, pot_ref)
    func_count, depth = refs[0].shape[-2:]
    atoms = owner_ref.shape[0]
    low_edge, high_edge = edges(func_count, depth)
    for a, (owner, rank) in enumerate(ranks(owner_ref, count_ref)):
        both = kernel_ref[rows_place(owner, sizes)].astype(jnp.float32)
        rows_ref[a : a + 1, :] = jnp.where(rank == 0, both[0:1], both[1:2])
    width = 9 * func_count
    matrix = jnp.concatenate([rows_ref[:, :width], rows_ref[:, width:]], axis=0)
    for copy in copies:
        copy.wait()
    for side_x, side_y in SIDES:
        at = (0, AT_X[side_x], AT_Y[side_y], AT_XY[side_x, side_y])
        left = jnp.concatenate(
            [matrix[:, k * func_count : (k + 1) * func_count] for k in at], axis=1
        ).astype(jnp.bfloat16)
        for at_x in range(half):
            for at_y in range(0, half, 2):
                right = jnp.concatenate(
                    [
                        jnp.concatenate(boxes.columns((side_x, side_y), at_x, y), axis=0)
                        for y in (at_y, at_y + 1)
                    ],
                    axis=1,
                )
                got = jnp.dot(left, right, preferred_element_type=jnp.float32)
                for i in (0, 1):
                    mixed_ref[side_x * half + at_x, side_y * half + at_y + i] = got[
                        :, i * depth : (i + 1) * depth
                    ]

    def cell(x, y):
        return mixed_ref[x, y]

    for x in range(2 * half):
        made = [
            stencil(cell, boxes.potential, half, x, y, low_edge, high_edge) for y in range(2 * half)
        ]
        for odd in (0, 1):
            stacked = jnp.stack([m[odd * atoms : (odd + 1) * atoms] for m in made], axis=0)
            out_ref[:, odd, x] = jnp.swapaxes(stacked, 0, 1).astype(out_ref.dtype)


def body(sizes, potential, functions, kernel_store, owners):
    own_funcs = functions[0, 0]
    func_count, ext_x, ext_y, depth = own_funcs.shape
    half = ext_x // 2
    margin = (ext_x - potential.shape[0]) // 2
    device_count = sizes[0] * sizes[1] * sizes[2] * sizes[3]
    owner_col = owners[:, 0]
    atoms = owner_col.shape[0]
    slot_count, row_width = kernel_store.shape
    slot_cap = slot_count // device_count
    bf16 = jnp.bfloat16
    struct = jax.ShapeDtypeStruct

    band = struct((2 * half * half + 1, func_count, depth), bf16)

    def split(kernel, *operands):
        return pl.pallas_call(
            functools.partial(kernel, half),
            out_shape=(band,) * 2,
            in_specs=[VMEM] * len(operands),
            out_specs=(VMEM,) * 2,
            compiler_params=params(),
            cost_estimate=pl.CostEstimate(flops=0, transcendentals=0, bytes_accessed=2 << 20),
        )(*operands)

    own_x = split(split_x_kernel, own_funcs, potential)
    from_x = (shifted(own_x[1], BRICK, 1), shifted(own_x[0], BRICK, -1))
    own_y = split(split_y_kernel, *own_x, potential)
    from_y = (shifted(own_y[1], NARROW, 1), shifted(own_y[0], NARROW, -1))
    kernel_store, *_ = lax.optimization_barrier((kernel_store, *own_y))
    kernel_out = pl.pallas_call(
        functools.partial(pair_kernel, sizes),
        out_shape=struct((device_count, slot_cap, row_width), bf16),
        in_specs=[VMEM],
        out_specs=VMEM,
        compiler_params=params(),
        cost_estimate=pl.CostEstimate(flops=0, transcendentals=0, bytes_accessed=1 << 20),
    )(kernel_store)
    kernel_in = lax.all_to_all(
        kernel_out, ROWS_ORDER, split_axis=0, concat_axis=0, tiled=True
    )

    count = half * half
    bands = lax.optimization_barrier((*from_x, *own_y, kernel_out))[:2]
    corners = [bands[sx][: count + 1] if sy else bands[sx][count:] for sx, sy in SIDES]
    from_xy = [shifted(c, NARROW, -1 if sy else 1) for c, (sx, sy) in zip(corners, SIDES)]

    boxes = (*own_x, *bands, *from_y, *from_xy)
    anywhere = pl.BlockSpec(memory_space=pltpu.HBM)
    cells = ext_x * ext_y * depth
    lines = 2 * slot_cap * (row_width // depth + 1)
    outgoing = pl.pallas_call(
        functools.partial(pairs_kernel, half, slot_cap, sizes),
        out_shape=struct((device_count, lines, depth), jnp.int16),
        in_specs=[SMEM] + [VMEM] * 11,
        out_specs=VMEM,
        scratch_shapes=[
            pltpu.VMEM((device_count, lines, depth), jnp.float32),
            pltpu.VMEM((pl.cdiv(9 * func_count, depth), 2 * func_count, depth), jnp.float32),
            pltpu.SMEM((device_count,), jnp.int32),
        ],
        compiler_params=params(60),
        cost_estimate=pl.CostEstimate(
            flops=16 * func_count * func_count * cells, transcendentals=0, bytes_accessed=7 << 20
        ),
    )(owner_col, potential, *boxes)
    blocks = lax.all_to_all(outgoing, ORDER, split_axis=0, concat_axis=0, tiled=True)
    steps = 2
    chunk = device_count // steps
    blocks = pl.pallas_call(
        functools.partial(unpack_kernel, slot_cap, sizes),
        grid=(steps,),
        out_shape=struct((slot_count, 2, row_width), jnp.float32),
        in_specs=[VMEM],
        out_specs=pl.BlockSpec((chunk * slot_cap, 2, row_width), lambda i: (i, 0, 0)),
        compiler_params=params(),
    )(blocks)

    gradient = pl.pallas_call(
        functools.partial(mix_kernel, half, sizes),
        out_shape=struct((atoms, 2, ext_x, ext_y, depth), bf16),
        in_specs=[SMEM, VMEM, VMEM] + [anywhere] * 10,
        out_specs=VMEM,
        scratch_shapes=[
            pltpu.VMEM((atoms, row_width), jnp.float32),
            pltpu.VMEM((ext_x, ext_y, func_count, depth), jnp.float32),
            pltpu.SMEM((device_count,), jnp.int32),
            pltpu.SemaphoreType.DMA((10,)),
        ]
        + [pltpu.VMEM(box.shape, box.dtype) for box in boxes],
        compiler_params=params(60),
        cost_estimate=pl.CostEstimate(
            flops=8 * func_count * func_count * cells, transcendentals=0, bytes_accessed=7 << 20
        ),
    )(owner_col, kernel_in, potential, *boxes)
    return (blocks, gradient.reshape(functions.shape))


def solution(mesh):
    sizes = (mesh.shape["brick"] // 4, 4, mesh.shape["narrow"] // 2, 2)
    mesh = Mesh(mesh.devices.reshape(sizes), BRICK + NARROW)
    every = BRICK + NARROW
    in_specs = (P(BRICK, NARROW, None), P(BRICK, NARROW, None, None, None, None), P(every, None), P(every, None))
    out_specs = (P(every, None, None), P(BRICK, NARROW, None, None, None, None))
    return jax.shard_map(
        functools.partial(body, sizes), mesh=mesh, in_specs=in_specs, out_specs=out_specs, check_vma=False
    )
```

```python
import functools

import jax
import jax.numpy as jnp
from jax import lax
from jax.experimental import pallas as pl
from jax.experimental.pallas import tpu as pltpu
from jax.sharding import Mesh
from jax.sharding import PartitionSpec as P

AT_X = {1: 1, 0: 2}
AT_Y = {1: 3, 0: 4}
AT_XY = {(1, 1): 5, (1, 0): 6, (0, 1): 7, (0, 0): 8}
SIDES = ((0, 0), (0, 1), (1, 0), (1, 1))
STEPS = 64.0
TOP = 32700.0
SMALLEST = 1e-33
VMEM = pl.BlockSpec(memory_space=pltpu.VMEM)
SMEM = pl.BlockSpec(memory_space=pltpu.SMEM)


BRICK, NARROW = ("z", "y"), ("x", "core")
ORDER = ("core", "x", "y", "z")
ROWS_ORDER = ("y", "core", "x", "z")


def place(device, sizes):
    z_bits, y_bits, x_bits, core_bits = (size.bit_length() - 1 for size in sizes)
    core = device & (sizes[3] - 1)
    x = (device >> core_bits) & (sizes[2] - 1)
    y = (device >> (core_bits + x_bits)) & (sizes[1] - 1)
    z = device >> (core_bits + x_bits + y_bits)
    return (((((core << x_bits) + x) << y_bits) + y) << z_bits) + z


def rows_place(device, sizes):
    z_bits, y_bits, x_bits, core_bits = (size.bit_length() - 1 for size in sizes)
    core = device & (sizes[3] - 1)
    x = (device >> core_bits) & (sizes[2] - 1)
    y = (device >> (core_bits + x_bits)) & (sizes[1] - 1)
    z = device >> (core_bits + x_bits + y_bits)
    return (((((y << core_bits) + core) << x_bits) + x) << z_bits) + z


def shifted(shard, axis, by):
    size = lax.axis_size(axis)
    return lax.ppermute(shard, axis, [(i, (i + by) % size) for i in range(size)])


def params(mib=16):
    return pltpu.CompilerParams(vmem_limit_bytes=mib << 20)


def packed_rows(rows, func_count):
    value = jnp.concatenate(rows, axis=0)
    pieces = []
    for _ in range(3):
        piece = value.astype(jnp.bfloat16).astype(jnp.float32)
        pieces.append(piece)
        value = value - piece
    count = func_count - 3 * len(rows)
    pieces.append(jnp.zeros((count, value.shape[1]), jnp.float32))
    return jnp.concatenate(pieces, axis=0).astype(jnp.bfloat16)


def unpacked_rows(block, count):
    block = block.astype(jnp.float32)
    return block[:count] + block[count : 2 * count] + block[2 * count : 3 * count]


def split_x_kernel(half, f_ref, pot_ref, *out_refs):
    count = half * half
    func_count = f_ref.shape[0]
    inner = pot_ref.shape[0]
    margin = half - inner // 2
    for x in range(2 * half):
        rows = jnp.swapaxes(f_ref[:, x], 0, 1)
        side, at = divmod(x, half)
        for y in (0, 1):
            start = y * (count + 1) + at * half
            out_refs[side][start : start + half] = rows[y * half : (y + 1) * half]
    for side in (0, 1):
        first = side * (inner - margin)
        out_refs[side][count] = packed_rows(
            [pot_ref[first + i, j : j + 1] for i in range(margin) for j in range(inner)], func_count
        )


def split_y_kernel(half, x0_ref, x1_ref, pot_ref, *out_refs):
    count = half * half
    func_count = x0_ref.shape[1]
    inner = pot_ref.shape[0]
    margin = half - inner // 2
    for side in (0, 1):
        for side_x, x_ref in enumerate((x0_ref, x1_ref)):
            start, taken = side_x * (count + 1), side * (count + 1)
            out_refs[side][start : start + count] = x_ref[taken : taken + count]
        first = side * (inner - margin)
        out_refs[side][count] = packed_rows(
            [pot_ref[i, first + j : first + j + 1] for i in range(inner) for j in range(margin)], func_count
        )


class Boxes:
    def __init__(self, half, refs, pot_ref):
        self.half, self.count = half, half * half
        self.own, self.x, self.y, self.xy = refs[0:2], refs[2:4], refs[4:6], dict(zip(SIDES, refs[6:10]))
        self.pot = pot_ref
        self.inner = pot_ref.shape[0]
        self.margin = half - self.inner // 2
        self.edge = {}

    def columns(self, sides, at_x, at_y):
        side_x, side_y = sides
        at = at_x * self.half + at_y
        return [
            self.own[side_x][side_y * (self.count + 1) + at],
            self.x[side_x][side_y * (self.count + 1) + at],
            self.y[side_y][side_x * (self.count + 1) + at],
            self.xy[sides][1 - side_y + at],
        ]

    def edge_row(self, key, row):
        if key not in self.edge:
            ref = self.xy[key] if isinstance(key, tuple) and key in self.xy else getattr(self, key[0])[key[1]]
            at = self.count
            if key in self.xy:
                at = self.count * key[1]
            self.edge[key] = unpacked_rows(ref[at], self.margin * self.inner)
        return self.edge[key][row : row + 1]

    def potential(self, x, y):
        inner, margin = self.inner, self.margin
        in_x, in_y = (margin <= v < margin + inner for v in (x, y))
        side_x, side_y = x // self.half, y // self.half
        near_x, near_y = x - side_x * (margin + inner), y - side_y * (margin + inner)
        if in_x and in_y:
            return self.pot[x - margin, y - margin : y - margin + 1]
        if in_y:
            return self.edge_row(("x", side_x), near_x * inner + y - margin)
        if in_x:
            return self.edge_row(("y", side_y), (x - margin) * margin + near_y)
        column = near_y if side_y else inner - margin + near_y
        return self.edge_row((side_x, side_y), near_x * inner + column)


def pair_kernel(sizes, k_ref, o_ref):
    z_size, y_size, x_size, core_size = sizes
    _, cap, width = o_ref.shape
    count = x_size * core_size * cap
    for z in range(z_size):
        start = pl.multiple_of((z * y_size + pl.program_id(0)) * count, count)
        rows = k_ref[pl.ds(start, count)].reshape(x_size, core_size, cap, width)
        for core in range(core_size):
            for x in range(x_size):
                o_ref[(core * x_size + x) * z_size + z] = rows[x, core]


def stencil(cell, potential_row, half, x, y, zero_low, zero_high):
    value = cell(x, y)
    beside = jnp.where(zero_high, 0.0, pltpu.roll(value, value.shape[1] - 1, 1)) + jnp.where(
        zero_low, 0.0, pltpu.roll(value, 1, 1)
    )
    for near_x, near_y in ((x + 1, y), (x - 1, y), (x, y + 1), (x, y - 1)):
        if 0 <= near_x < 2 * half and 0 <= near_y < 2 * half:
            beside = beside + cell(near_x, near_y)
    return (3.0 + potential_row(x, y)) * value - 0.5 * beside


def edges(func_count, depth):
    lane = lax.broadcasted_iota(jnp.int32, (func_count, depth), 1)
    return lane == 0, lane == depth - 1


def ranks(owner_ref, count_ref):
    def clear(i, carry):
        count_ref[owner_ref[i]] = 0
        return carry

    lax.fori_loop(0, owner_ref.shape[0], clear, 0)
    found = []
    for a in range(owner_ref.shape[0]):
        owner = owner_ref[a]
        rank = count_ref[owner]
        count_ref[owner] = rank + 1
        found.append((owner, rank))
    return found


def pairs_kernel(half, cap, sizes, owner_ref, pot_ref, *refs):
    out_ref, wide_ref, sums_ref, count_ref = refs[10:14]
    boxes = Boxes(half, refs[0:10], pot_ref)
    func_count, depth = refs[0].shape[-2:]
    atoms = owner_ref.shape[0]
    low_edge, high_edge = edges(func_count, depth)

    def cell(x, y):
        side_x, at_x = divmod(x, half)
        side_y, at_y = divmod(y, half)
        return boxes.columns((side_x, side_y), at_x, at_y)[0].astype(jnp.float32)

    wide_ref[...] = jnp.zeros(wide_ref.shape, wide_ref.dtype)
    block = {}
    for side_x, side_y in SIDES:
        total = jnp.zeros((2 * func_count, 4 * func_count), jnp.float32)
        for at_x in range(half):
            left, right = [], []
            for at_y in range(half):
                columns = boxes.columns((side_x, side_y), at_x, at_y)
                applied = stencil(
                    cell, boxes.potential, half, side_x * half + at_x, side_y * half + at_y, low_edge, high_edge
                ).astype(jnp.bfloat16)
                left.append(jnp.concatenate([columns[0], applied], axis=0))
                right.append(jnp.concatenate(columns, axis=0))
            total = total + lax.dot_general(
                jnp.concatenate(left, axis=1),
                jnp.concatenate(right, axis=1),
                (((1,), (1,)), ((), ())),
                preferred_element_type=jnp.float32,
            )
        block[side_x, side_y] = total

    def summed(part, *sides):
        return functools.reduce(
            jnp.add, [block[s][:, part * func_count : (part + 1) * func_count] for s in sides]
        )

    parts = [summed(0, *SIDES)] + [None] * 8
    for side in (0, 1):
        parts[AT_X[side]] = summed(1, (side, 0), (side, 1))
        parts[AT_Y[side]] = summed(2, (0, side), (1, side))
    for sides in SIDES:
        parts[AT_XY[sides]] = summed(3, sides)
    width = 9 * func_count
    volume = 1.0 / (4 * half * half * depth)
    sums = jnp.concatenate(parts, axis=1) * volume
    for t in range(0, width, depth):
        sums_ref[t // depth, :, : min(depth, width - t)] = sums[:, t : t + depth]

    def atom_rows(start):
        picked = []
        for i in (0, 1):
            tiles = [sums_ref[t, pl.ds(start + i, atoms, stride=2), :] for t in range(sums_ref.shape[0])]
            picked.append(jnp.concatenate(tiles, axis=1)[:, :width])
        return jnp.concatenate(picked, axis=1)

    coded = []
    for start in (0, func_count):
        row = atom_rows(start)
        largest = jnp.maximum(jnp.max(jnp.abs(row), axis=1, keepdims=True), SMALLEST)
        power = jnp.ceil(STEPS * jnp.log2(largest))
        coded.append((row * (TOP * jnp.exp2(-power / STEPS)), jnp.broadcast_to(power, (atoms, depth))))
    tiles = 2 * width // depth
    for a, (owner, rank) in enumerate(ranks(owner_ref, count_ref)):
        at = place(owner, sizes)
        for m, (row, power) in enumerate(coded):
            for t in range(tiles):
                wide_ref[at, pl.ds(rank * (2 * tiles) + 2 * t + m, 1), :] = row[
                    a : a + 1, t * depth : (t + 1) * depth
                ]
            wide_ref[at, pl.ds(cap * 2 * tiles + 2 * rank + m, 1), :] = power[a : a + 1]
    for owner in range(out_ref.shape[0]):
        out_ref[owner] = jnp.round(wide_ref[owner]).astype(jnp.int32).astype(jnp.int16)


def unpack_kernel(cap, sizes, in_ref, out_ref):
    chunks = out_ref.shape[0] // cap
    _, rows, depth = in_ref.shape
    data = rows - 2 * cap
    line = lax.broadcasted_iota(jnp.int32, (data, depth), 0)
    even = line % 2 == 0
    for c in range(chunks):
        at = place(c, sizes) + pl.program_id(0) * (chunks * sizes[0] // in_ref.shape[0])
        values = in_ref[at].astype(jnp.int32).astype(jnp.float32)
        scale = jnp.exp2(values[data:] * (1.0 / STEPS)) * (1.0 / TOP)
        spread = jnp.where(even, scale[0:1], scale[1:2])
        for rank in range(1, cap):
            spread = jnp.where(
                line >= rank * (data // cap),
                jnp.where(even, scale[2 * rank : 2 * rank + 1], scale[2 * rank + 1 : 2 * rank + 2]),
                spread,
            )
        values = values[:data] * spread
        for rank in range(cap):
            for t in range(data // (2 * cap)):
                start = rank * (data // cap) + 2 * t
                out_ref[c * cap + rank, :, t * depth : (t + 1) * depth] = values[start : start + 2]


def mix_kernel(half, sizes, owner_ref, kernel_ref, pot_ref, *refs):
    out_ref, rows_ref, mixed_ref, count_ref, sems = refs[10:15]
    held = refs[15:25]
    copies = [pltpu.make_async_copy(refs[i], held[i], sems.at[i]) for i in range(10)]
    for copy in copies:
        copy.start()
    boxes = Boxes(half, held, pot_ref)
    func_count, depth = refs[0].shape[-2:]
    atoms = owner_ref.shape[0]
    low_edge, high_edge = edges(func_count, depth)
    for a, (owner, rank) in enumerate(ranks(owner_ref, count_ref)):
        both = kernel_ref[rows_place(owner, sizes)].astype(jnp.float32)
        rows_ref[a : a + 1, :] = jnp.where(rank == 0, both[0:1], both[1:2])
    width = 9 * func_count
    matrix = jnp.concatenate([rows_ref[:, :width], rows_ref[:, width:]], axis=0)
    for copy in copies:
        copy.wait()
    for side_x, side_y in SIDES:
        at = (0, AT_X[side_x], AT_Y[side_y], AT_XY[side_x, side_y])
        left = jnp.concatenate(
            [matrix[:, k * func_count : (k + 1) * func_count] for k in at], axis=1
        ).astype(jnp.bfloat16)
        for at_x in range(half):
            for at_y in range(0, half, 2):
                right = jnp.concatenate(
                    [
                        jnp.concatenate(boxes.columns((side_x, side_y), at_x, y), axis=0)
                        for y in (at_y, at_y + 1)
                    ],
                    axis=1,
                )
                got = jnp.dot(left, right, preferred_element_type=jnp.float32)
                for i in (0, 1):
                    mixed_ref[side_x * half + at_x, side_y * half + at_y + i] = got[
                        :, i * depth : (i + 1) * depth
                    ]

    def cell(x, y):
        return mixed_ref[x, y]

    for x in range(2 * half):
        made = [
            stencil(cell, boxes.potential, half, x, y, low_edge, high_edge) for y in range(2 * half)
        ]
        for odd in (0, 1):
            stacked = jnp.stack([m[odd * atoms : (odd + 1) * atoms] for m in made], axis=0)
            out_ref[:, odd, x] = jnp.swapaxes(stacked, 0, 1).astype(out_ref.dtype)


def body(sizes, potential, functions, kernel_store, owners):
    own_funcs = functions[0, 0]
    func_count, ext_x, ext_y, depth = own_funcs.shape
    half = ext_x // 2
    margin = (ext_x - potential.shape[0]) // 2
    device_count = sizes[0] * sizes[1] * sizes[2] * sizes[3]
    owner_col = owners[:, 0]
    atoms = owner_col.shape[0]
    slot_count, row_width = kernel_store.shape
    slot_cap = slot_count // device_count
    bf16 = jnp.bfloat16
    struct = jax.ShapeDtypeStruct

    band = struct((2 * half * half + 1, func_count, depth), bf16)

    def split(kernel, *operands):
        return pl.pallas_call(
            functools.partial(kernel, half),
            out_shape=(band,) * 2,
            in_specs=[VMEM] * len(operands),
            out_specs=(VMEM,) * 2,
            compiler_params=params(),
            cost_estimate=pl.CostEstimate(flops=0, transcendentals=0, bytes_accessed=2 << 20),
        )(*operands)

    own_x = split(split_x_kernel, own_funcs, potential)
    from_x = (shifted(own_x[1], BRICK, 1), shifted(own_x[0], BRICK, -1))
    own_y = split(split_y_kernel, *own_x, potential)
    from_y = (shifted(own_y[1], NARROW, 1), shifted(own_y[0], NARROW, -1))
    kernel_store, *_ = lax.optimization_barrier((kernel_store, *own_y))
    kernel_out = pl.pallas_call(
        functools.partial(pair_kernel, sizes),
        out_shape=struct((device_count, slot_cap, row_width), bf16),
        in_specs=[VMEM],
        out_specs=pl.BlockSpec((device_count // sizes[1], slot_cap, row_width), lambda i: (i, 0, 0)),
        grid=(sizes[1],),
        compiler_params=params(),
        cost_estimate=pl.CostEstimate(flops=0, transcendentals=0, bytes_accessed=1 << 20),
    )(kernel_store)
    kernel_in = lax.all_to_all(
        kernel_out, ROWS_ORDER, split_axis=0, concat_axis=0, tiled=True
    )

    count = half * half
    bands = lax.optimization_barrier((*from_x, *own_y, kernel_out))[:2]
    corners = [bands[sx][: count + 1] if sy else bands[sx][count:] for sx, sy in SIDES]
    from_xy = [shifted(c, NARROW, -1 if sy else 1) for c, (sx, sy) in zip(corners, SIDES)]

    boxes = (*own_x, *bands, *from_y, *from_xy)
    anywhere = pl.BlockSpec(memory_space=pltpu.HBM)
    cells = ext_x * ext_y * depth
    lines = 2 * slot_cap * (row_width // depth + 1)
    outgoing = pl.pallas_call(
        functools.partial(pairs_kernel, half, slot_cap, sizes),
        out_shape=struct((device_count, lines, depth), jnp.int16),
        in_specs=[SMEM] + [VMEM] * 11,
        out_specs=VMEM,
        scratch_shapes=[
            pltpu.VMEM((device_count, lines, depth), jnp.float32),
            pltpu.VMEM((pl.cdiv(9 * func_count, depth), 2 * func_count, depth), jnp.float32),
            pltpu.SMEM((device_count,), jnp.int32),
        ],
        compiler_params=params(60),
        cost_estimate=pl.CostEstimate(
            flops=16 * func_count * func_count * cells, transcendentals=0, bytes_accessed=7 << 20
        ),
    )(owner_col, potential, *boxes)
    blocks = lax.all_to_all(outgoing, ORDER, split_axis=0, concat_axis=0, tiled=True)
    steps = 2
    chunk = device_count // steps
    blocks = pl.pallas_call(
        functools.partial(unpack_kernel, slot_cap, sizes),
        grid=(steps,),
        out_shape=struct((slot_count, 2, row_width), jnp.float32),
        in_specs=[VMEM],
        out_specs=pl.BlockSpec((chunk * slot_cap, 2, row_width), lambda i: (i, 0, 0)),
        compiler_params=params(),
    )(blocks)

    gradient = pl.pallas_call(
        functools.partial(mix_kernel, half, sizes),
        out_shape=struct((atoms, 2, ext_x, ext_y, depth), bf16),
        in_specs=[SMEM, VMEM, VMEM] + [anywhere] * 10,
        out_specs=VMEM,
        scratch_shapes=[
            pltpu.VMEM((atoms, row_width), jnp.float32),
            pltpu.VMEM((ext_x, ext_y, func_count, depth), jnp.float32),
            pltpu.SMEM((device_count,), jnp.int32),
            pltpu.SemaphoreType.DMA((10,)),
        ]
        + [pltpu.VMEM(box.shape, box.dtype) for box in boxes],
        compiler_params=params(60),
        cost_estimate=pl.CostEstimate(
            flops=8 * func_count * func_count * cells, transcendentals=0, bytes_accessed=7 << 20
        ),
    )(owner_col, kernel_in, potential, *boxes)
    return (blocks, gradient.reshape(functions.shape))


def solution(mesh):
    sizes = (mesh.shape["brick"] // 4, 4, mesh.shape["narrow"] // 2, 2)
    mesh = Mesh(mesh.devices.reshape(sizes), BRICK + NARROW)
    every = BRICK + NARROW
    in_specs = (P(BRICK, NARROW, None), P(BRICK, NARROW, None, None, None, None), P(every, None), P(every, None))
    out_specs = (P(every, None, None), P(BRICK, NARROW, None, None, None, None))
    return jax.shard_map(
        functools.partial(body, sizes), mesh=mesh, in_specs=in_specs, out_specs=out_specs, check_vma=False
    )
```
